256 devices in a mesh: leaf: 64 (over x, z, core), rhs: 4 (over y).
Axes of the slice: x: 4, y: 4, z: 8, core: 2. Of those that a mesh axis runs over, the one named last changes fastest.
Arguments:
- rhs_vectors: bfloat16 [32, 131072], P('rhs', 'leaf'), may hold values from -6 to 6
- diag_inverse: bfloat16 [131072, 2048], P('leaf'), may hold values from -1 to 2
- left_factors: bfloat16 [131072, 384], P('leaf'), may hold values from -0.125 to 0.125
- right_factors: bfloat16 [131072, 384], P('leaf'), may hold values from -0.125 to 0.125
- ranks: int32 [6], replicated, may hold values from 32 to 64, as said below
Outputs:
- solution: float32 [32, 131072], P('rhs', 'leaf')
The draws below stay inside these ranges and needn't reach their ends.
Inputs may be any that keep to these rules, and one draw needn't show every extreme that they name: `ranks`: some level has rank exactly 64.
All inputs are finite; a program needn't handle non-finite values.
Results may differ from the reference program's by a relative error of at most 0.0031.
Values sent between devices are 32-bit elements; how exact they have to be, the bound alone decides.
No kernel may reach another device: no remote copies, remote signals or barrier semaphores. Data moves between devices by JAX's collectives and lax.ppermute only.
A program may use at most 64 MiB of HBM per device.

```python
import math
import jax
import jax.numpy as jnp
from jax import lax

M = 2048
RMAX = 64
LEVELS = 6
UNKNOWNS = 131072
NRHS = 32
N_LEAF = 64


def draw_diag_inverse(key, part):
    noise = jnp.clip(jax.random.normal(key, (UNKNOWNS, M), jnp.float32), -4.0, 4.0)
    row_id = lax.broadcasted_iota(jnp.int32, (UNKNOWNS, M), 0) % M
    col_id = lax.broadcasted_iota(jnp.int32, (UNKNOWNS, M), 1)
    eye_block = jnp.where(row_id == col_id, 1.0, 0.0).astype(jnp.float32)
    return (eye_block + noise * (0.5 / math.sqrt(M))).astype(jnp.bfloat16)


def draw_ranks(key, part):
    picks = jax.random.randint(jax.random.fold_in(key, 11), (LEVELS,), RMAX // 2, RMAX + 1)
    chosen = jax.random.randint(jax.random.fold_in(key, 12), (), 0, LEVELS)
    slots = lax.broadcasted_iota(jnp.int32, (LEVELS,), 0)
    return jnp.where(slots == chosen, RMAX, picks).astype(jnp.int32)


def shard_levels(key, extent, split, least, largest):
    factor_of = 1.0
    for dim, blocks in split:
        draws = jax.random.uniform(jax.random.fold_in(jax.random.fold_in(key, 6), dim), (blocks,), jnp.float32, least / len(split), largest / len(split))
        factor_of = factor_of * jnp.repeat(jnp.exp(draws), extent[dim] // blocks).reshape((-1,) + (1,) * (len(extent) - 1 - dim))
    return factor_of


def centred(key, shape, width, most, pieces=(), held_as=jnp.bfloat16):
    factor_of = shard_levels(key, shape, pieces, -0.22, 0.18) if pieces else 1.0
    result = jax.random.normal(key, shape, jnp.float32) * width * factor_of
    return jnp.minimum(jnp.maximum(result, -most), most).astype(held_as)


def setup_inputs(seed: int = 0) -> dict:
    arg_keys = jax.random.split(jax.random.key(seed), 6)
    return {
        "rhs_vectors": centred(arg_keys[0], (NRHS, UNKNOWNS), 1.0, 6.0, ((0, 4), (1, 64))),
        "diag_inverse": draw_diag_inverse(jax.random.fold_in(arg_keys[5], 71), 0),
        "left_factors": centred(arg_keys[2], (UNKNOWNS, LEVELS * RMAX), (RMAX * N_LEAF // 2) ** -0.5, 0.125, ((0, 64),)),
        "right_factors": centred(arg_keys[3], (UNKNOWNS, LEVELS * RMAX), M ** -0.5, 0.125, ((0, 64),)),
        "ranks": draw_ranks(jax.random.fold_in(arg_keys[5], 71), 0),
    }


best_precision = lax.Precision.HIGHEST


def reference(rhs_vectors, diag_inverse, left_factors, right_factors, ranks):
    state_rows = LEVELS * RMAX
    column_level = jnp.arange(state_rows) // RMAX
    column_rank = jnp.arange(state_rows) % RMAX
    level_table = jnp.arange(LEVELS)
    rank_of = jnp.sum(jnp.where(column_level[:, None] == level_table[None, :], ranks[None, :], 0), axis=1)
    column_keep = (column_rank < rank_of).astype(jnp.bfloat16)
    rhs_count = rhs_vectors.shape[0]
    solved = []
    projections = []
    for leaf_pos in range(N_LEAF):
        lower_row = leaf_pos * M
        inverse = diag_inverse[lower_row:lower_row + M]
        left_kept = left_factors[lower_row:lower_row + M] * column_keep[None, :]
        right_kept = (right_factors[lower_row:lower_row + M] * column_keep[None, :]).astype(jnp.float32)
        mapped = jnp.dot(inverse, left_kept, preferred_element_type=jnp.float32).astype(jnp.bfloat16)
        source = rhs_vectors[:, lower_row:lower_row + M].T
        base = jnp.dot(inverse, source, preferred_element_type=jnp.float32)
        incoming = jnp.zeros((state_rows, rhs_count), jnp.float32)
        for tree_level in range(LEVELS):
            if (leaf_pos >> tree_level) & 1:
                first_leaf = (leaf_pos >> (tree_level + 1)) << (tree_level + 1)
                gathered = projections[first_leaf]
                for sibling in range(first_leaf + 1, first_leaf + (1 << tree_level)):
                    gathered = gathered + projections[sibling]
                low_edge = tree_level * RMAX
                incoming = incoming.at[low_edge:low_edge + RMAX].set(gathered[low_edge:low_edge + RMAX])
        answer = base - jnp.dot(mapped.astype(jnp.float32), incoming, precision=best_precision)
        projections.append(jnp.dot(right_kept.T, answer, precision=best_precision))
        solved.append(answer.T)
    return jnp.concatenate(solved, axis=1)
```

```python
import jax
import jax.numpy as jnp
from jax import lax
from jax.experimental import pallas as pl
from jax.experimental.pallas import tpu as pltpu
from jax.sharding import PartitionSpec as P

f32 = jnp.float32
bf16 = jnp.bfloat16
NN = (((1,), (0,)), ((), ()))
NT = (((1,), (1,)), ((), ()))
RANK = 64
LEVELS = 6
STATE = RANK * LEVELS
CHUNK = 512
PARTNER = (1, 2, 4, 12, 16, 48)


def mul(a, b, dims=NN):
    return lax.dot_general(a, b, dims, preferred_element_type=f32)


def halves(x):
    high = x.astype(bf16)
    return high, (x - high.astype(f32)).astype(bf16)


def thirds(x):
    high, low = halves(x)
    rest = x - high.astype(f32) - low.astype(f32)
    return high, low, rest.astype(bf16)


def wide_mul(a, b):
    a_high, a_low = halves(a)
    b_high, b_low = halves(b)
    return mul(
        jnp.concatenate([a_high, a_high, a_low], axis=1),
        jnp.concatenate([b_high, b_low, b_high], axis=0),
    )


def upper(level):
    return (lax.axis_index("leaf") >> level & 1) == 1


def side_by_side(x, blocks):
    return jnp.concatenate([x[RANK * j : RANK * (j + 1)] for j in range(blocks)], axis=1)


def stacked(x, blocks):
    return jnp.concatenate([x[:, RANK * j : RANK * (j + 1)] for j in range(blocks)], axis=0)


def outgoing(level, state, send):
    blocks = LEVELS - 1 - level
    is_upper = upper(level)
    if level == LEVELS - 1:
        send[...] = jnp.concatenate([state[RANK:, RANK : 2 * RANK]] * 2, axis=1)
    elif level % 2 == 0:
        pivot = state[:RANK, RANK:]
        packed = jnp.concatenate([stacked(pivot, blocks), state[RANK * (blocks + 1) :, :RANK]], axis=0)
        first = jnp.where(is_upper, packed, state[RANK:, :RANK])
        send[:, : 2 * RANK] = jnp.concatenate([first, state[RANK:, RANK : 2 * RANK]], axis=1)
        if blocks > 1:
            send[:, 2 * RANK :] = state[RANK:, 2 * RANK :]
    else:
        rows = RANK * blocks + 8
        send[:rows] = state[RANK:, 2 * RANK :]
        left = state[RANK:, RANK : 2 * RANK]
        packed = side_by_side(left, blocks)
        send[rows : rows + RANK] = jnp.where(is_upper, state[:RANK, 2 * RANK :], packed)
        send[rows + RANK :] = jnp.concatenate([left[RANK * blocks :]] * blocks, axis=1)


def pivots(level, got):
    blocks = LEVELS - 1 - level
    if level % 2 == 0:
        return got[:, :RANK]
    rows = RANK * blocks + 8
    return jnp.concatenate([stacked(got[rows : rows + RANK], blocks), got[rows + RANK :, :RANK]], axis=0)


def first_kernel(ranks, b_hbm, d_hbm, u_hbm, v_hbm, mapped, base, state, send, d, u, v, b, x, acc, sems):
    size = d.shape[0]
    n = size // CHUNK
    copies = [
        pltpu.make_async_copy(d_hbm.at[pl.ds(CHUNK * i, CHUNK)], d.at[pl.ds(CHUNK * i, CHUNK)], sems.at[i])
        for i in range(n)
    ]
    copy_u = pltpu.make_async_copy(u_hbm, u, sems.at[n])
    copy_b = pltpu.make_async_copy(b_hbm, b, sems.at[n + 1])
    copy_v = pltpu.make_async_copy(v_hbm, v, sems.at[n + 2])
    copy_u.start()
    copy_b.start()
    copies[0].start()
    copy_v.start()
    for c in copies[1:]:
        c.start()
    lane = lax.broadcasted_iota(jnp.int32, (1, STATE), 1)
    keep = jnp.zeros((1, STATE), f32)
    for level in range(LEVELS):
        inside = (lane >= RANK * level) & (lane < RANK * level + jnp.minimum(ranks[level], RANK))
        keep = jnp.where(inside, 1.0, keep)
    copy_u.wait()
    copy_b.wait()
    x[:STATE] = (u[...] * keep.astype(bf16)).T
    x[STATE:] = jnp.concatenate([b[...], jnp.zeros((8, size), bf16)], axis=0)
    for i in range(n):
        rows = slice(CHUNK * i, CHUNK * (i + 1))
        copies[i].wait()
        if i == 0:
            copy_v.wait()
        product = mul(x[...], d[rows], NT)
        rounded = product[:STATE].astype(bf16)
        mapped[:, rows] = rounded
        part = product[STATE : STATE + 8]
        base[:, rows] = part
        joined = jnp.concatenate([rounded, *thirds(part)], axis=0)
        total = mul(joined, v[rows])
        if i == 0:
            acc[...] = total
        else:
            acc[...] += total
    state[:STATE] = acc[:STATE] * keep
    state[STATE:] = (acc[STATE : STATE + 8] + acc[STATE + 8 : STATE + 16] + acc[STATE + 16 :]) * keep
    outgoing(0, state[...], send)


def level_kernel(level, own, got, state, send):
    blocks = LEVELS - 1 - level
    is_upper = upper(level)
    skip = RANK if level % 2 else 0
    first = 2 * skip
    own_left = own[RANK:, skip : skip + RANK]
    own_right = own[:RANK, first:]
    arrived = got[...]
    left = jnp.where(is_upper, pivots(level, arrived), own_left)
    if level % 2 == 0:
        bulk = arrived
        right = jnp.concatenate([own_right[:, :RANK], side_by_side(arrived[:, :RANK], blocks)], axis=1)
    else:
        rows = RANK * blocks + 8
        bulk = arrived[:rows]
        right = arrived[rows : rows + RANK]
    right = jnp.where(is_upper, own_right, right)
    state[...] = own[RANK:, first:] + bulk - wide_mul(left, right)
    outgoing(level + 1, state[...], send)


def coefficients(level, got, t):
    blocks = LEVELS - 1 - level
    left = jnp.where(upper(level), pivots(level, got), 0.0)
    done = -left
    if t is None:
        return done
    done = jnp.concatenate([t[RANK:] - wide_mul(left, t[:RANK]), done], axis=1)
    return done


def coefficient_kernel(levels, *refs):
    count = len(levels)
    t = refs[count][...] if len(refs) == count + 2 else None
    for level, got in zip(levels, refs):
        t = coefficients(level, got[...], t)
    refs[-1][...] = t


def basis_kernel(got, t_ref, mapped, base, out):
    t = coefficients(3, got[...], t_ref[...])
    w = mapped[...]
    high, low = halves(t)
    rows = t.shape[0]
    product = mul(jnp.concatenate([high, low], axis=0), w[: t.shape[1]])
    product = product[:rows] + product[rows:]
    out[: 2 * RANK] = w[4 * RANK :].astype(f32) + product[: 2 * RANK]
    out[2 * RANK :] = base[...] + product[2 * RANK :]


def late_kernel(got, basis, high_low, shifted):
    left = jnp.where(upper(4), pivots(4, got[...]), 0.0)
    update = basis[RANK:] - wide_mul(left, basis[:RANK])
    high, low = halves(update[:RANK])
    high_low[:RANK] = high
    high_low[RANK : 2 * RANK] = low
    high_low[2 * RANK :] = high
    shifted[...] = update[RANK:]


def last_kernel(got, high_low, shifted, out):
    value = jnp.where(upper(5), got[:, :RANK], 0.0)
    high, low = halves(value)
    out[...] = shifted[...] - mul(jnp.concatenate([high, high, low], axis=1), high_low[...])


def send_shape(level):
    blocks = LEVELS - 1 - level
    if level == LEVELS - 1:
        return (8, 2 * RANK)
    if level % 2 == 0:
        return (RANK * blocks + 8, RANK * (blocks + 1))
    return (RANK * (blocks + 1) + 16, RANK * blocks)


def state_shape(level):
    return (RANK * (LEVELS - level) + 8, STATE - 2 * RANK * (level // 2))


def call(kernel, name, outs, *args):
    vmem = pl.BlockSpec(memory_space=pltpu.VMEM)
    return pl.pallas_call(
        kernel,
        name=name,
        in_specs=[vmem] * len(args),
        out_specs=[vmem] * len(outs),
        out_shape=[jax.ShapeDtypeStruct(s, t) for s, t in outs],
    )(*args)


def on_device(rhs_vectors, diag_inverse, left_factors, right_factors, ranks):
    size = diag_inverse.shape[0]
    vmem = pl.BlockSpec(memory_space=pltpu.VMEM)
    hbm = pl.BlockSpec(memory_space=pl.ANY)
    mapped, base, state, send = pl.pallas_call(
        first_kernel,
        name="first",
        in_specs=[pl.BlockSpec(memory_space=pltpu.SMEM), hbm, hbm, hbm, hbm],
        out_specs=[vmem] * 4,
        out_shape=[
            jax.ShapeDtypeStruct((STATE, size), bf16),
            jax.ShapeDtypeStruct((8, size), f32),
            jax.ShapeDtypeStruct(state_shape(0), f32),
            jax.ShapeDtypeStruct(send_shape(0), f32),
        ],
        scratch_shapes=[
            pltpu.VMEM((size, size), bf16),
            pltpu.VMEM((size, STATE), bf16),
            pltpu.VMEM((size, STATE), bf16),
            pltpu.VMEM((8, size), bf16),
            pltpu.VMEM((STATE + 16, size), bf16),
            pltpu.VMEM((STATE + 24, STATE), f32),
            pltpu.SemaphoreType.DMA((size // CHUNK + 3,)),
        ],
    )(ranks, rhs_vectors, diag_inverse, left_factors, right_factors)
    got = []
    t = None
    for level in range(LEVELS):
        pairs = [(i, i ^ PARTNER[level]) for i in range(lax.axis_size("leaf"))]
        got.append(lax.ppermute(send, "leaf", pairs))
        if level < LEVELS - 1:
            state, send = call(
                lambda *refs, level=level: level_kernel(level, *refs),
                f"level_{level}",
                [(state_shape(level + 1), f32), (send_shape(level + 1), f32)],
                state,
                got[level],
            )
    (t,) = call(
        lambda *refs: coefficient_kernel((0, 1, 2), *refs),
        "coefficients",
        [((3 * RANK + 8, 3 * RANK), f32)],
        *got[:3],
    )
    (basis,) = call(basis_kernel, "basis", [((2 * RANK + 8, size), f32)], got[3], t, mapped, base)
    high_low, shifted = call(late_kernel, "late", [((3 * RANK, size), bf16), ((8, size), f32)], got[4], basis)
    (out,) = call(last_kernel, "last", [((8, size), f32)], got[5], high_low, shifted)
    return out


def solution(mesh):
    in_specs = (P("rhs", "leaf"), P("leaf", None), P("leaf", None), P("leaf", None), P())
    out_specs = P("rhs", "leaf")
    return jax.shard_map(
        on_device, mesh=mesh, in_specs=in_specs, out_specs=out_specs, check_vma=False
    )
```

```python
import jax
import jax.numpy as jnp
from jax import lax
from jax.experimental import pallas as pl
from jax.experimental.pallas import tpu as pltpu
from jax.sharding import PartitionSpec as P

f32 = jnp.float32
bf16 = jnp.bfloat16
NN = (((1,), (0,)), ((), ()))
NT = (((1,), (1,)), ((), ()))
RANK = 64
LEVELS = 6
STATE = RANK * LEVELS
CHUNK = 512
PARTNER = (1, 2, 4, 12, 16, 48)


def mul(a, b, dims=NN):
    return lax.dot_general(a, b, dims, preferred_element_type=f32)


def halves(x):
    high = x.astype(bf16)
    return high, (x - high.astype(f32)).astype(bf16)


def thirds(x):
    high, low = halves(x)
    rest = x - high.astype(f32) - low.astype(f32)
    return high, low, rest.astype(bf16)


def wide_mul(a, b):
    a_high, a_low = halves(a)
    b_high, b_low = halves(b)
    return mul(
        jnp.concatenate([a_high, a_high, a_low], axis=1),
        jnp.concatenate([b_high, b_low, b_high], axis=0),
    )


def upper(level):
    return (lax.axis_index("leaf") >> level & 1) == 1


def side_by_side(x, blocks):
    return jnp.concatenate([x[RANK * j : RANK * (j + 1)] for j in range(blocks)], axis=1)


def stacked(x, blocks):
    return jnp.concatenate([x[:, RANK * j : RANK * (j + 1)] for j in range(blocks)], axis=0)


def outgoing(level, state, send):
    blocks = LEVELS - 1 - level
    is_upper = upper(level)
    if level == LEVELS - 1:
        send[...] = jnp.concatenate([state[RANK:, RANK : 2 * RANK]] * 2, axis=1)
    elif level % 2 == 0:
        pivot = state[:RANK, RANK:]
        packed = jnp.concatenate([stacked(pivot, blocks), state[RANK * (blocks + 1) :, :RANK]], axis=0)
        first = jnp.where(is_upper, packed, state[RANK:, :RANK])
        send[:, : 2 * RANK] = jnp.concatenate([first, state[RANK:, RANK : 2 * RANK]], axis=1)
        if blocks > 1:
            send[:, 2 * RANK :] = state[RANK:, 2 * RANK :]
    else:
        rows = RANK * blocks + 8
        send[:rows] = state[RANK:, 2 * RANK :]
        left = state[RANK:, RANK : 2 * RANK]
        packed = side_by_side(left, blocks)
        send[rows : rows + RANK] = jnp.where(is_upper, state[:RANK, 2 * RANK :], packed)
        send[rows + RANK :] = jnp.concatenate([left[RANK * blocks :]] * blocks, axis=1)


def pivots(level, got):
    blocks = LEVELS - 1 - level
    if level % 2 == 0:
        return got[:, :RANK]
    rows = RANK * blocks + 8
    return jnp.concatenate([stacked(got[rows : rows + RANK], blocks), got[rows + RANK :, :RANK]], axis=0)


def first_kernel(ranks, b_hbm, d_hbm, u_hbm, v_hbm, mapped, base, state, send, d, u, v, b, x, acc, sems):
    size = d.shape[0]
    n = size // CHUNK
    copies = [
        pltpu.make_async_copy(d_hbm.at[pl.ds(CHUNK * i, CHUNK)], d.at[pl.ds(CHUNK * i, CHUNK)], sems.at[i])
        for i in range(n)
    ]
    copy_u = pltpu.make_async_copy(u_hbm, u, sems.at[n])
    copy_b = pltpu.make_async_copy(b_hbm, b, sems.at[n + 1])
    copy_v = pltpu.make_async_copy(v_hbm, v, sems.at[n + 2])
    copy_u.start()
    copy_b.start()
    copies[0].start()
    copy_v.start()
    for c in copies[1:]:
        c.start()
    lane = lax.broadcasted_iota(jnp.int32, (1, STATE), 1)
    keep = jnp.zeros((1, STATE), f32)
    for level in range(LEVELS):
        inside = (lane >= RANK * level) & (lane < RANK * level + jnp.minimum(ranks[level], RANK))
        keep = jnp.where(inside, 1.0, keep)
    copy_u.wait()
    copy_b.wait()
    x[:STATE] = (u[...] * keep.astype(bf16)).T
    x[STATE:] = jnp.concatenate([b[...], jnp.zeros((8, size), bf16)], axis=0)
    for i in range(n):
        rows = slice(CHUNK * i, CHUNK * (i + 1))
        copies[i].wait()
        if i == 0:
            copy_v.wait()
        product = mul(x[...], d[rows], NT)
        rounded = product[:STATE].astype(bf16)
        mapped[:, rows] = rounded
        part = product[STATE : STATE + 8]
        base[:, rows] = part
        joined = jnp.concatenate([rounded, *thirds(part)], axis=0)
        total = mul(joined, v[rows])
        if i == 0:
            acc[...] = total
        else:
            acc[...] += total
    state[:STATE] = acc[:STATE] * keep
    state[STATE:] = (acc[STATE : STATE + 8] + acc[STATE + 8 : STATE + 16] + acc[STATE + 16 :]) * keep
    outgoing(0, state[...], send)


def level_kernel(level, own, got, *refs):
    send = refs[-1]
    blocks = LEVELS - 1 - level
    is_upper = upper(level)
    skip = RANK if level % 2 else 0
    first = 2 * skip
    own_left = own[RANK:, skip : skip + RANK]
    own_right = own[:RANK, first:]
    arrived = got[...]
    left = jnp.where(is_upper, pivots(level, arrived), own_left)
    if level % 2 == 0:
        bulk = arrived
        right = jnp.concatenate([own_right[:, :RANK], side_by_side(arrived[:, :RANK], blocks)], axis=1)
    else:
        rows = RANK * blocks + 8
        bulk = arrived[:rows]
        right = arrived[rows : rows + RANK]
    right = jnp.where(is_upper, own_right, right)
    total = own[RANK:, first:] + bulk - wide_mul(left, right)
    if level < LEVELS - 2:
        refs[-2][...] = total
    outgoing(level + 1, total, send)


def coefficients(level, got, t):
    blocks = LEVELS - 1 - level
    left = jnp.where(upper(level), pivots(level, got), 0.0)
    done = -left
    if t is None:
        return done
    done = jnp.concatenate([t[RANK:] - wide_mul(left, t[:RANK]), done], axis=1)
    return done


def coefficient_kernel(levels, *refs):
    count = len(levels)
    t = refs[count][...] if len(refs) == count + 2 else None
    for level, got in zip(levels, refs):
        t = coefficients(level, got[...], t)
    refs[-1][...] = t


def basis_kernel(got, t_ref, mapped, base, out):
    t = coefficients(3, got[...], t_ref[...])
    w = mapped[...]
    high, low = halves(t)
    rows = t.shape[0]
    product = mul(jnp.concatenate([high, low], axis=0), w[: t.shape[1]])
    product = product[:rows] + product[rows:]
    out[: 2 * RANK] = w[4 * RANK :].astype(f32) + product[: 2 * RANK]
    out[2 * RANK :] = base[...] + product[2 * RANK :]


def late_kernel(got, basis, high_low, shifted):
    left = jnp.where(upper(4), pivots(4, got[...]), 0.0)
    update = basis[RANK:] - wide_mul(left, basis[:RANK])
    high, low = halves(update[:RANK])
    high_low[:RANK] = high
    high_low[RANK : 2 * RANK] = low
    high_low[2 * RANK :] = high
    shifted[...] = update[RANK:]


def last_kernel(got, high_low, shifted, out):
    value = jnp.where(upper(5), got[:, :RANK], 0.0)
    high, low = halves(value)
    out[...] = shifted[...] - mul(jnp.concatenate([high, high, low], axis=1), high_low[...])


def send_shape(level):
    blocks = LEVELS - 1 - level
    if level == LEVELS - 1:
        return (8, 2 * RANK)
    if level % 2 == 0:
        return (RANK * blocks + 8, RANK * (blocks + 1))
    return (RANK * (blocks + 1) + 16, RANK * blocks)


def state_shape(level):
    return (RANK * (LEVELS - level) + 8, STATE - 2 * RANK * (level // 2))


def call(kernel, name, outs, *args, after=()):
    vmem = pl.BlockSpec(memory_space=pltpu.VMEM)
    count = len(args)

    def body(*refs):
        kernel(*refs[:count], *refs[count + len(after) :])

    return pl.pallas_call(
        body,
        name=name,
        in_specs=[vmem] * count + [pl.BlockSpec(memory_space=pl.ANY)] * len(after),
        out_specs=[vmem] * len(outs),
        out_shape=[jax.ShapeDtypeStruct(s, t) for s, t in outs],
        compiler_params=pltpu.CompilerParams(vmem_limit_bytes=16 << 20),
    )(*args, *after)


def on_device(rhs_vectors, diag_inverse, left_factors, right_factors, ranks):
    size = diag_inverse.shape[0]
    vmem = pl.BlockSpec(memory_space=pltpu.VMEM)
    hbm = pl.BlockSpec(memory_space=pltpu.HBM)
    mapped, base, state, send = pl.pallas_call(
        first_kernel,
        name="first",
        in_specs=[pl.BlockSpec(memory_space=pltpu.SMEM), hbm, hbm, hbm, hbm],
        out_specs=[vmem] * 4,
        out_shape=[
            jax.ShapeDtypeStruct((STATE, size), bf16),
            jax.ShapeDtypeStruct((8, size), f32),
            jax.ShapeDtypeStruct(state_shape(0), f32),
            jax.ShapeDtypeStruct(send_shape(0), f32),
        ],
        scratch_shapes=[
            pltpu.VMEM((size, size), bf16),
            pltpu.VMEM((size, STATE), bf16),
            pltpu.VMEM((size, STATE), bf16),
            pltpu.VMEM((8, size), bf16),
            pltpu.VMEM((STATE + 16, size), bf16),
            pltpu.VMEM((STATE + 24, STATE), f32),
            pltpu.SemaphoreType.DMA((size // CHUNK + 3,)),
        ],
        compiler_params=pltpu.CompilerParams(vmem_limit_bytes=40 << 20),
    )(
        *(
            pltpu.with_memory_space_constraint(a, pltpu.HBM)
            for a in (ranks, rhs_vectors, diag_inverse, left_factors, right_factors)
        ),
    )
    got = []
    for level in range(LEVELS):
        pairs = [(i, i ^ PARTNER[level]) for i in range(lax.axis_size("leaf"))]
        got.append(lax.ppermute(send, "leaf", pairs))
        after = ()
        if level == 3:
            (t,) = after = call(
                lambda *refs: coefficient_kernel((0, 1, 2), *refs),
                "coefficients",
                [((3 * RANK + 8, 3 * RANK), f32)],
                *got[:3],
            )
        if level == 4:
            (basis,) = after = call(
                basis_kernel, "basis", [((2 * RANK + 8, size), f32)], got[3], t, mapped, base
            )
        if level < LEVELS - 1:
            outs = [(send_shape(level + 1), f32)]
            if level < LEVELS - 2:
                outs.insert(0, (state_shape(level + 1), f32))
            *states, send = call(
                lambda *refs, level=level: level_kernel(level, *refs),
                f"level_{level}",
                outs,
                state,
                got[level],
                after=after,
            )
            state = states[0] if states else None
    high_low, shifted = call(late_kernel, "late", [((3 * RANK, size), bf16), ((8, size), f32)], got[4], basis)
    (out,) = call(last_kernel, "last", [((8, size), f32)], got[5], high_low, shifted)
    return out


def solution(mesh):
    in_specs = (P("rhs", "leaf"), P("leaf", None), P("leaf", None), P("leaf", None), P())
    out_specs = P("rhs", "leaf")
    return jax.shard_map(
        on_device, mesh=mesh, in_specs=in_specs, out_specs=out_specs, check_vma=False
    )
```

```python
import jax
import jax.numpy as jnp
from jax import lax
from jax.experimental import pallas as pl
from jax.experimental.pallas import tpu as pltpu
from jax.sharding import PartitionSpec as P

f32 = jnp.float32
bf16 = jnp.bfloat16
NN = (((1,), (0,)), ((), ()))
NT = (((1,), (1,)), ((), ()))
RANK = 64
LEVELS = 6
STATE = RANK * LEVELS
CHUNK = 512
PARTNER = (1, 2, 4, 12, 16, 48)
SPLIT = (1, 2, 3)


def mul(a, b, dims=NN):
    return lax.dot_general(a, b, dims, preferred_element_type=f32)


def halves(x):
    high = x.astype(bf16)
    return high, (x - high.astype(f32)).astype(bf16)


def thirds(x):
    high, low = halves(x)
    rest = x - high.astype(f32) - low.astype(f32)
    return high, low, rest.astype(bf16)


def wide_mul(a, b):
    a_high, a_low = halves(a)
    b_high, b_low = halves(b)
    return mul(
        jnp.concatenate([a_high, a_high, a_low], axis=1),
        jnp.concatenate([b_high, b_low, b_high], axis=0),
    )


def upper(level):
    return (lax.axis_index("leaf") >> level & 1) == 1


def side_by_side(x, blocks):
    return jnp.concatenate([x[RANK * j : RANK * (j + 1)] for j in range(blocks)], axis=1)


def stacked(x, blocks):
    return jnp.concatenate([x[:, RANK * j : RANK * (j + 1)] for j in range(blocks)], axis=0)


def outgoing(level, state):
    blocks = LEVELS - 1 - level
    is_upper = upper(level)
    if level == LEVELS - 1:
        return jnp.concatenate([state[RANK:, RANK : 2 * RANK]] * 2, axis=1)
    if level % 2 == 0:
        packed = jnp.concatenate([stacked(state[:RANK, RANK:], blocks), state[RANK * (blocks + 1) :, :RANK]], axis=0)
        first = jnp.where(is_upper, packed, state[RANK:, :RANK])
        tiles = [jnp.concatenate([first, state[RANK:, RANK : 2 * RANK]], axis=1)]
        if blocks > 1:
            tiles.append(state[RANK:, 2 * RANK :])
        message = jnp.concatenate(tiles, axis=1)
    else:
        left = state[RANK:, RANK : 2 * RANK]
        pivot = jnp.where(is_upper, state[:RANK, 2 * RANK :], side_by_side(left, blocks))
        rest = jnp.concatenate([left[RANK * blocks :]] * blocks, axis=1)
        message = jnp.concatenate([state[RANK:, 2 * RANK :], pivot, rest], axis=0)
    short = whole_rows(level) - message.shape[0]
    if short:
        message = jnp.concatenate([message, jnp.zeros((short, message.shape[1]), f32)], axis=0)
    return message


def post(level, state, send, full):
    message = outgoing(level, state)
    if level in SPLIT:
        full[...] = message
        half = send.shape[0]
        send[...] = full[pl.ds(half * (lax.axis_index("leaf") & 1), half)]
    else:
        send[...] = message


def pivots(level, got):
    blocks = LEVELS - 1 - level
    rows = RANK * blocks + 8
    if level % 2 == 0:
        return got[:rows, :RANK]
    return jnp.concatenate([stacked(got[rows : rows + RANK], blocks), got[rows + RANK :, :RANK]], axis=0)


def first_kernel(ranks, b_hbm, d_hbm, u_hbm, v_hbm, mapped, base, state, send, d, u, v, b, x, acc, sems):
    size = d.shape[0]
    n = size // CHUNK
    copies = [
        pltpu.make_async_copy(d_hbm.at[pl.ds(CHUNK * i, CHUNK)], d.at[pl.ds(CHUNK * i, CHUNK)], sems.at[i])
        for i in range(n)
    ]
    copy_u = pltpu.make_async_copy(u_hbm, u, sems.at[n])
    copy_b = pltpu.make_async_copy(b_hbm, b, sems.at[n + 1])
    copy_v = pltpu.make_async_copy(v_hbm, v, sems.at[n + 2])
    copy_u.start()
    copy_b.start()
    copies[0].start()
    copy_v.start()
    for c in copies[1:]:
        c.start()
    lane = lax.broadcasted_iota(jnp.int32, (1, STATE), 1)
    keep = jnp.zeros((1, STATE), f32)
    for level in range(LEVELS):
        inside = (lane >= RANK * level) & (lane < RANK * level + jnp.minimum(ranks[level], RANK))
        keep = jnp.where(inside, 1.0, keep)
    copy_u.wait()
    copy_b.wait()
    x[:STATE] = (u[...] * keep.astype(bf16)).T
    x[STATE:] = jnp.concatenate([b[...], jnp.zeros((8, size), bf16)], axis=0)
    for i in range(n):
        rows = slice(CHUNK * i, CHUNK * (i + 1))
        copies[i].wait()
        if i == 0:
            copy_v.wait()
        product = mul(x[...], d[rows], NT)
        rounded = product[:STATE].astype(bf16)
        mapped[:, rows] = rounded
        part = product[STATE : STATE + 8]
        base[:, rows] = part
        joined = jnp.concatenate([rounded, *thirds(part)], axis=0)
        total = mul(joined, v[rows])
        if i == 0:
            acc[...] = total
        else:
            acc[...] += total
    state[:STATE] = acc[:STATE] * keep
    state[STATE:] = (acc[STATE : STATE + 8] + acc[STATE + 8 : STATE + 16] + acc[STATE + 16 :]) * keep
    post(0, state[...], send, None)


def level_kernel(level, *refs):
    parts = 2 if level in SPLIT else 1
    own, got, refs = refs[0], refs[1 : 1 + parts], list(refs[1 + parts :])
    received, sent = refs[-2:]
    blocks = LEVELS - 1 - level
    rows = RANK * blocks + 8
    is_upper = upper(level)
    if parts == 2:
        half = got[0].shape[0]
        core = lax.axis_index("leaf") & 1
        received[pl.ds(half * core, half)] = got[0][...]
        received[pl.ds(half * (1 - core), half)] = got[1][...]
        arrived = received[...]
    else:
        arrived = got[0][...]
    skip = RANK if level % 2 else 0
    first = 2 * skip
    own_left = own[RANK:, skip : skip + RANK]
    own_right = own[:RANK, first:]
    theirs = pivots(level, arrived)
    left = jnp.where(is_upper, theirs, own_left)
    bulk = arrived[:rows]
    if level % 2 == 0:
        right = jnp.concatenate([own_right[:, :RANK], side_by_side(arrived[:, :RANK], blocks)], axis=1)
    else:
        right = arrived[rows : rows + RANK]
    right = jnp.where(is_upper, own_right, right)
    total = own[RANK:, first:] + bulk - wide_mul(left, right)
    post(level + 1, total, refs[0], sent)
    refs[1][...] = jnp.where(is_upper, theirs, 0.0)
    if level < LEVELS - 2:
        refs[2][...] = total


def coefficients(left, t):
    if t is None:
        return -left
    return jnp.concatenate([t[RANK:] - wide_mul(left, t[:RANK]), -left], axis=1)


def coefficient_kernel(*refs):
    t = None
    for left in refs[:-1]:
        t = coefficients(left[...], t)
    refs[-1][...] = t


def basis_kernel(left, t_ref, mapped, base, out):
    t = coefficients(left[...], t_ref[...])
    w = mapped[...]
    high, low = halves(t)
    rows = t.shape[0]
    product = mul(jnp.concatenate([high, low], axis=0), w[: t.shape[1]])
    product = product[:rows] + product[rows:]
    out[: 2 * RANK] = w[4 * RANK :].astype(f32) + product[: 2 * RANK]
    out[2 * RANK :] = base[...] + product[2 * RANK :]


def late_kernel(left, basis, high_low, shifted):
    update = basis[RANK:] - wide_mul(left[...], basis[:RANK])
    high, low = halves(update[:RANK])
    high_low[:RANK] = high
    high_low[RANK : 2 * RANK] = low
    high_low[2 * RANK :] = high
    shifted[...] = update[RANK:]


def last_kernel(got, high_low, shifted, out):
    value = jnp.where(upper(5), got[:, :RANK], 0.0)
    high, low = halves(value)
    out[...] = shifted[...] - mul(jnp.concatenate([high, high, low], axis=1), high_low[...])


def whole_rows(level):
    blocks = LEVELS - 1 - level
    if level == LEVELS - 1:
        return 8
    rows = RANK * blocks + 8 if level % 2 == 0 else RANK * (blocks + 1) + 16
    return -(-rows // 16) * 16 if level in SPLIT else rows


def whole_shape(level):
    blocks = LEVELS - 1 - level
    if level == LEVELS - 1:
        return (8, 2 * RANK)
    return (whole_rows(level), RANK * (blocks + 1 - level % 2))


def send_shape(level):
    rows, lanes = whole_shape(level)
    return (rows // 2 if level in SPLIT else rows, lanes)


def state_shape(level):
    return (RANK * (LEVELS - level) + 8, STATE - 2 * RANK * (level // 2))


def call(kernel, name, outs, *args, after=(), scratch=()):
    vmem = pl.BlockSpec(memory_space=pltpu.VMEM)
    count = len(args)

    def body(*refs):
        kernel(*refs[:count], *refs[count + len(after) :])

    return pl.pallas_call(
        body,
        name=name,
        in_specs=[vmem] * count + [pl.BlockSpec(memory_space=pl.ANY)] * len(after),
        out_specs=[vmem] * len(outs),
        out_shape=[jax.ShapeDtypeStruct(s, t) for s, t in outs],
        scratch_shapes=[pltpu.VMEM(s, f32) for s in scratch],
        compiler_params=pltpu.CompilerParams(vmem_limit_bytes=16 << 20),
    )(*args, *after)


def swapped(x, distance):
    return lax.ppermute(x, "leaf", [(i, i ^ distance) for i in range(lax.axis_size("leaf"))])


def on_device(rhs_vectors, diag_inverse, left_factors, right_factors, ranks):
    size = diag_inverse.shape[0]
    vmem = pl.BlockSpec(memory_space=pltpu.VMEM)
    hbm = pl.BlockSpec(memory_space=pltpu.HBM)
    mapped, base, state, send = pl.pallas_call(
        first_kernel,
        name="first",
        in_specs=[pl.BlockSpec(memory_space=pltpu.SMEM), hbm, hbm, hbm, hbm],
        out_specs=[vmem] * 4,
        out_shape=[
            jax.ShapeDtypeStruct((STATE, size), bf16),
            jax.ShapeDtypeStruct((8, size), f32),
            jax.ShapeDtypeStruct(state_shape(0), f32),
            jax.ShapeDtypeStruct(send_shape(0), f32),
        ],
        scratch_shapes=[
            pltpu.VMEM((size, size), bf16),
            pltpu.VMEM((size, STATE), bf16),
            pltpu.VMEM((size, STATE), bf16),
            pltpu.VMEM((8, size), bf16),
            pltpu.VMEM((STATE + 16, size), bf16),
            pltpu.VMEM((STATE + 24, STATE), f32),
            pltpu.SemaphoreType.DMA((size // CHUNK + 3,)),
        ],
        compiler_params=pltpu.CompilerParams(vmem_limit_bytes=40 << 20),
    )(
        *(
            pltpu.with_memory_space_constraint(a, pltpu.HBM)
            for a in (ranks, rhs_vectors, diag_inverse, left_factors, right_factors)
        ),
    )
    lefts = []
    basis = t = None
    for level in range(LEVELS - 1):
        got = [swapped(send, PARTNER[level])]
        if level in SPLIT:
            got.append(swapped(got[0], 1))
        after = ()
        if level == 3:
            (t,) = after = call(coefficient_kernel, "coefficients", [((3 * RANK + 8, 3 * RANK), f32)], *lefts)
        if level == 4:
            (basis,) = after = call(
                basis_kernel, "basis", [((2 * RANK + 8, size), f32)], lefts[3], t, mapped, base
            )
        outs = [send_shape(level + 1), (RANK * (LEVELS - 1 - level) + 8, RANK)]
        if level < LEVELS - 2:
            outs.append(state_shape(level + 1))
        send, left, *state = call(
            lambda *refs, level=level: level_kernel(level, *refs),
            f"level_{level}",
            [(s, f32) for s in outs],
            state,
            *got,
            after=after,
            scratch=[whole_shape(level), whole_shape(level + 1)],
        )
        state = state[0] if state else None
        lefts.append(left)
    got = swapped(send, PARTNER[LEVELS - 1])
    high_low, shifted = call(
        late_kernel, "late", [((3 * RANK, size), bf16), ((8, size), f32)], lefts[4], basis
    )
    (out,) = call(last_kernel, "last", [((8, size), f32)], got, high_low, shifted)
    return out


def solution(mesh):
    in_specs = (P("rhs", "leaf"), P("leaf", None), P("leaf", None), P("leaf", None), P())
    out_specs = P("rhs", "leaf")
    return jax.shard_map(
        on_device, mesh=mesh, in_specs=in_specs, out_specs=out_specs, check_vma=False
    )
```

```python
import jax
import jax.numpy as jnp
from jax import lax
from jax.experimental import pallas as pl
from jax.experimental.pallas import tpu as pltpu
from jax.sharding import PartitionSpec as P

f32 = jnp.float32
bf16 = jnp.bfloat16
NN = (((1,), (0,)), ((), ()))
NT = (((1,), (1,)), ((), ()))
RANK = 64
LEVELS = 6
STATE = RANK * LEVELS
CHUNK = 512
PARTNER = (1, 2, 4, 12, 16, 48)
PIECES = (9, 6, 4, 2, 1, 0)


def mul(a, b, dims=NN):
    return lax.dot_general(a, b, dims, preferred_element_type=f32)


def halves(x):
    high = x.astype(bf16)
    return high, (x - high.astype(f32)).astype(bf16)


def thirds(x):
    high, low = halves(x)
    rest = x - high.astype(f32) - low.astype(f32)
    return high, low, rest.astype(bf16)


def wide_mul(a, b):
    a_high, a_low = halves(a)
    b_high, b_low = halves(b)
    return mul(
        jnp.concatenate([a_high, a_high, a_low], axis=1),
        jnp.concatenate([b_high, b_low, b_high], axis=0),
    )


def upper(level):
    return (lax.axis_index("leaf") >> level & 1) == 1


def folded(x):
    return jnp.concatenate([x[: RANK // 2], x[RANK // 2 :]], axis=1)


def unfolded(x):
    return jnp.concatenate([x[:, :RANK], x[:, RANK:]], axis=0)


class Places:
    def __init__(self, level):
        self.count = LEVELS - 1 - level
        leaf = lax.axis_index("leaf")
        self.bits = [(leaf >> (level + 1 + k)) & 1 for k in range(self.count)]
        self.ones_before = [sum(self.bits[:k], jnp.int32(0)) for k in range(self.count + 1)]
        self.ones = self.ones_before[-1]
        self.zeros = self.count - self.ones
        self.inner = self.ones * self.zeros

    def next_piece(self, position):
        own = self.bits[0]
        ones, zeros = self.ones - own, self.zeros - (1 - own)
        inner = ones * zeros
        within = position < inner
        a = sum([(position >= t * zeros).astype(jnp.int32) for t in range(1, self.count)], jnp.int32(0))
        b = position - a * zeros
        rest = position - inner
        a = jnp.where(within, a + own, jnp.where(own == 1, 0, rest))
        b = jnp.where(within, b + 1 - own, jnp.where(own == 1, rest, 0))
        valid = (a < self.ones) & (b < self.zeros)
        return jnp.where(valid, a, 0), jnp.where(valid, b, 0), valid

    def nth(self, n, bit):
        found = jnp.int32(0)
        for k in range(self.count):
            before = self.ones_before[k] if bit else k - self.ones_before[k]
            found = jnp.where((before == n) & (self.bits[k] == bit), k, found)
        return found


def piece(ref, index, limit):
    index = jnp.minimum(index, limit - 1)
    return ref[pl.ds(pl.multiple_of(RANK // 2 * index, RANK // 2), RANK // 2)]


def first_kernel(ranks, b_hbm, d_hbm, u_hbm, v_hbm, mapped, base, send, d, u, v, b, x, acc, keeps, sems):
    size = d.shape[0]
    n = size // CHUNK
    copies = [
        pltpu.make_async_copy(d_hbm.at[pl.ds(CHUNK * i, CHUNK)], d.at[pl.ds(CHUNK * i, CHUNK)], sems.at[i])
        for i in range(n)
    ]
    copy_u = pltpu.make_async_copy(u_hbm, u, sems.at[n])
    copy_b = pltpu.make_async_copy(b_hbm, b, sems.at[n + 1])
    copy_v = pltpu.make_async_copy(v_hbm, v, sems.at[n + 2])
    copy_u.start()
    copy_b.start()
    copies[0].start()
    copy_v.start()
    for c in copies[1:]:
        c.start()
    lane = lax.broadcasted_iota(jnp.int32, (1, STATE), 1)
    keep = jnp.zeros((1, STATE), f32)
    for level in range(LEVELS):
        inside = (lane >= RANK * level) & (lane < RANK * level + jnp.minimum(ranks[level], RANK))
        keep = jnp.where(inside, 1.0, keep)
    keeps[...] = jnp.broadcast_to(keep, keeps.shape)
    copy_u.wait()
    copy_b.wait()
    x[:STATE] = (u[...] * keep.astype(bf16)).T
    x[STATE:] = jnp.concatenate([b[...], jnp.zeros((8, size), bf16)], axis=0)
    for i in range(n):
        rows = slice(CHUNK * i, CHUNK * (i + 1))
        copies[i].wait()
        if i == 0:
            copy_v.wait()
        product = mul(x[...], d[rows], NT)
        rounded = product[:STATE].astype(bf16)
        mapped[:, rows] = rounded
        part = product[STATE : STATE + 8]
        base[:, rows] = part
        joined = jnp.concatenate([rounded, *thirds(part)], axis=0)
        total = mul(joined, v[rows])
        if i == 0:
            acc[...] = total
        else:
            acc[...] += total
    rhs = (acc[STATE : STATE + 8] + acc[STATE + 8 : STATE + 16] + acc[STATE + 16 :]) * keep
    places = Places(-1)
    for position in range(PIECES[0]):
        one, zero, valid = places.next_piece(position)
        m, lane_piece = places.nth(one, 1), places.nth(zero, 0)
        rows = pl.ds(pl.multiple_of(RANK * m, RANK), RANK)
        lanes = pl.ds(pl.multiple_of(2 * RANK * (lane_piece // 2), 2 * RANK), 2 * RANK)
        tile = acc[rows, lanes] * keeps[:1, lanes]
        block = jnp.where(lane_piece % 2 == 1, tile[:, RANK:], tile[:, :RANK])
        send[RANK // 2 * position : RANK // 2 * (position + 1)] = folded(jnp.where(valid, block, 0.0))
    for tile in range(LEVELS // 2):
        row = RANK // 2 * PIECES[0] + 8 * tile
        send[row : row + 8] = rhs[:, 2 * RANK * tile : 2 * RANK * (tile + 1)]


def level_kernel(level, own, got, send, left):
    places = Places(level)
    is_upper = upper(level)
    count = PIECES[level]
    rhs_row = RANK // 2 * count
    tiles = LEVELS // 2 - level // 2
    lower_of = lambda index: unfolded(
        jnp.where(is_upper, piece(got, index, count), piece(own, index, count))
    )
    upper_of = lambda index: unfolded(
        jnp.where(is_upper, piece(own, index, count), piece(got, index, count))
    )
    own_rhs = jnp.concatenate([own[rhs_row + 8 * t : rhs_row + 8 * t + 8] for t in range(tiles)], axis=1)
    got_rhs = jnp.concatenate([got[rhs_row + 8 * t : rhs_row + 8 * t + 8] for t in range(tiles)], axis=1)
    skip = RANK * (level % 2)
    pivot_rhs = jnp.where(is_upper, got_rhs, own_rhs)[:, skip : skip + RANK]
    for position in range(PIECES[level + 1]):
        one, zero, valid = places.next_piece(position)
        index = one * places.zeros + zero
        product = wide_mul(lower_of(places.inner + one), upper_of(places.inner + zero))
        block = piece(own, index, count) + piece(got, index, count) - folded(product)
        send[RANK // 2 * position : RANK // 2 * (position + 1)] = jnp.where(valid, block, 0.0)
    rights = []
    lefts = []
    for k in range(places.count):
        zeros_before = k - places.ones_before[k]
        right = upper_of(places.inner + zeros_before)
        rights.append(jnp.where(places.bits[k] == 0, right, 0.0))
        theirs = unfolded(piece(got, places.inner + places.ones_before[k], count))
        lefts.append(jnp.where(is_upper & (places.bits[k] == 1), theirs, 0.0))
    blank = jnp.zeros((RANK, RANK + skip), f32)
    product = wide_mul(pivot_rhs, jnp.concatenate([blank, *rights], axis=1))
    rhs = own_rhs + got_rhs - product
    skip_tiles = level % 2
    for t in range(skip_tiles, tiles):
        row = RANK // 2 * PIECES[level + 1] + 8 * (t - skip_tiles)
        send[row : row + 8] = rhs[:, 2 * RANK * t : 2 * RANK * (t + 1)]
    lefts.append(jnp.where(is_upper, pivot_rhs, 0.0))
    left[...] = jnp.concatenate(lefts, axis=0)


def coefficients(left, t):
    if t is None:
        return -left
    return jnp.concatenate([t[RANK:] - wide_mul(left, t[:RANK]), -left], axis=1)


def coefficient_kernel(*refs):
    t = None
    for left in refs[:-1]:
        t = coefficients(left[...], t)
    refs[-1][...] = t


def basis_kernel(left, t_ref, mapped, base, out):
    t = coefficients(left[...], t_ref[...])
    w = mapped[...]
    high, low = halves(t)
    rows = t.shape[0]
    product = mul(jnp.concatenate([high, low], axis=0), w[: t.shape[1]])
    product = product[:rows] + product[rows:]
    out[: 2 * RANK] = w[4 * RANK :].astype(f32) + product[: 2 * RANK]
    out[2 * RANK :] = base[...] + product[2 * RANK :]


def late_kernel(left, basis, high_low, shifted):
    update = basis[RANK:] - wide_mul(left[...], basis[:RANK])
    high, low = halves(update[:RANK])
    high_low[:RANK] = high
    high_low[RANK : 2 * RANK] = low
    high_low[2 * RANK :] = high
    shifted[...] = update[RANK:]


def last_kernel(got, high_low, shifted, out):
    value = jnp.where(upper(5), got[:, RANK:], 0.0)
    high, low = halves(value)
    out[...] = shifted[...] - mul(jnp.concatenate([high, high, low], axis=1), high_low[...])


def send_shape(level):
    return (RANK // 2 * PIECES[level] + 8 * (LEVELS // 2 - level // 2), 2 * RANK)


def call(kernel, name, outs, *args, after=()):
    vmem = pl.BlockSpec(memory_space=pltpu.VMEM)
    count = len(args)

    def body(*refs):
        kernel(*refs[:count], *refs[count + len(after) :])

    return pl.pallas_call(
        body,
        name=name,
        in_specs=[vmem] * count + [pl.BlockSpec(memory_space=pl.ANY)] * len(after),
        out_specs=[vmem] * len(outs),
        out_shape=[jax.ShapeDtypeStruct(s, t) for s, t in outs],
        compiler_params=pltpu.CompilerParams(vmem_limit_bytes=16 << 20),
    )(*args, *after)


def swapped(x, distance):
    return lax.ppermute(x, "leaf", [(i, i ^ distance) for i in range(lax.axis_size("leaf"))])


def on_device(rhs_vectors, diag_inverse, left_factors, right_factors, ranks):
    size = diag_inverse.shape[0]
    vmem = pl.BlockSpec(memory_space=pltpu.VMEM)
    hbm = pl.BlockSpec(memory_space=pltpu.HBM)
    mapped, base, send = pl.pallas_call(
        first_kernel,
        name="first",
        in_specs=[pl.BlockSpec(memory_space=pltpu.SMEM), hbm, hbm, hbm, hbm],
        out_specs=[vmem] * 3,
        out_shape=[
            jax.ShapeDtypeStruct((STATE, size), bf16),
            jax.ShapeDtypeStruct((8, size), f32),
            jax.ShapeDtypeStruct(send_shape(0), f32),
        ],
        scratch_shapes=[
            pltpu.VMEM((size, size), bf16),
            pltpu.VMEM((size, STATE), bf16),
            pltpu.VMEM((size, STATE), bf16),
            pltpu.VMEM((8, size), bf16),
            pltpu.VMEM((STATE + 16, size), bf16),
            pltpu.VMEM((STATE + 24, STATE), f32),
            pltpu.VMEM((8, STATE), f32),
            pltpu.SemaphoreType.DMA((size // CHUNK + 3,)),
        ],
        compiler_params=pltpu.CompilerParams(vmem_limit_bytes=40 << 20),
    )(
        *(
            pltpu.with_memory_space_constraint(a, pltpu.HBM)
            for a in (ranks, rhs_vectors, diag_inverse, left_factors, right_factors)
        ),
    )
    lefts = []
    basis = t = None
    for level in range(LEVELS - 1):
        got = swapped(send, PARTNER[level])
        after = ()
        if level == 3:
            (t,) = after = call(coefficient_kernel, "coefficients", [((3 * RANK + 8, 3 * RANK), f32)], *lefts)
        if level == 4:
            (basis,) = after = call(
                basis_kernel, "basis", [((2 * RANK + 8, size), f32)], lefts[3], t, mapped, base
            )
        send, left = call(
            lambda *refs, level=level: level_kernel(level, *refs),
            f"level_{level}",
            [(send_shape(level + 1), f32), ((RANK * (LEVELS - 1 - level) + 8, RANK), f32)],
            send,
            got,
            after=after,
        )
        lefts.append(left)
    got = swapped(send, PARTNER[LEVELS - 1])
    high_low, shifted = call(
        late_kernel, "late", [((3 * RANK, size), bf16), ((8, size), f32)], lefts[4], basis
    )
    (out,) = call(last_kernel, "last", [((8, size), f32)], got, high_low, shifted)
    return out


def solution(mesh):
    in_specs = (P("rhs", "leaf"), P("leaf", None), P("leaf", None), P("leaf", None), P())
    out_specs = P("rhs", "leaf")
    return jax.shard_map(
        on_device, mesh=mesh, in_specs=in_specs, out_specs=out_specs, check_vma=False
    )
```

```python
import jax
import jax.numpy as jnp
from jax import lax
from jax.experimental import pallas as pl
from jax.experimental.pallas import tpu as pltpu
from jax.sharding import PartitionSpec as P

f32 = jnp.float32
bf16 = jnp.bfloat16
NN = (((1,), (0,)), ((), ()))
NT = (((1,), (1,)), ((), ()))
RANK = 64
LEVELS = 6
STATE = RANK * LEVELS
CHUNK = 512
PARTNER = (1, 2, 4, 12)
PIECES = (9, 6, 4, 2, 1)


def mul(a, b, dims=NN):
    return lax.dot_general(a, b, dims, preferred_element_type=f32)


def halves(x):
    high = x.astype(bf16)
    return high, (x - high.astype(f32)).astype(bf16)


def thirds(x):
    high, low = halves(x)
    rest = x - high.astype(f32) - low.astype(f32)
    return high, low, rest.astype(bf16)


def wide_mul(a, b):
    a_high, a_low = halves(a)
    b_high, b_low = halves(b)
    return mul(
        jnp.concatenate([a_high, a_high, a_low], axis=1),
        jnp.concatenate([b_high, b_low, b_high], axis=0),
    )


def upper(level):
    return (lax.axis_index("leaf") >> level & 1) == 1


def folded(x):
    return jnp.concatenate([x[: RANK // 2], x[RANK // 2 :]], axis=1)


def unfolded(x):
    return jnp.concatenate([x[:, :RANK], x[:, RANK:]], axis=0)


class Places:
    def __init__(self, level):
        self.count = LEVELS - 1 - level
        leaf = lax.axis_index("leaf")
        self.bits = [(leaf >> (level + 1 + k)) & 1 for k in range(self.count)]
        self.ones_before = [sum(self.bits[:k], jnp.int32(0)) for k in range(self.count + 1)]
        self.ones = self.ones_before[-1]
        self.zeros = self.count - self.ones
        self.inner = self.ones * self.zeros

    def next_piece(self, position):
        own = self.bits[0]
        ones, zeros = self.ones - own, self.zeros - (1 - own)
        inner = ones * zeros
        within = position < inner
        a = sum([(position >= t * zeros).astype(jnp.int32) for t in range(1, self.count)], jnp.int32(0))
        b = position - a * zeros
        rest = position - inner
        a = jnp.where(within, a + own, jnp.where(own == 1, 0, rest))
        b = jnp.where(within, b + 1 - own, jnp.where(own == 1, rest, 0))
        valid = (a < self.ones) & (b < self.zeros)
        return jnp.where(valid, a, 0), jnp.where(valid, b, 0), valid

    def nth(self, n, bit):
        found = jnp.int32(0)
        for k in range(self.count):
            before = self.ones_before[k] if bit else k - self.ones_before[k]
            found = jnp.where((before == n) & (self.bits[k] == bit), k, found)
        return found


def piece(ref, index, limit):
    index = jnp.minimum(index, limit - 1)
    return ref[pl.ds(pl.multiple_of(RANK // 2 * index, RANK // 2), RANK // 2)]


def first_kernel(ranks, b_hbm, d_hbm, u_hbm, v_hbm, mapped, base, send, d, u, v, b, x, acc, keeps, sems):
    size = d.shape[0]
    n = size // CHUNK
    copies = [
        pltpu.make_async_copy(d_hbm.at[pl.ds(CHUNK * i, CHUNK)], d.at[pl.ds(CHUNK * i, CHUNK)], sems.at[i])
        for i in range(n)
    ]
    copy_u = pltpu.make_async_copy(u_hbm, u, sems.at[n])
    copy_b = pltpu.make_async_copy(b_hbm, b, sems.at[n + 1])
    copy_v = pltpu.make_async_copy(v_hbm, v, sems.at[n + 2])
    copy_u.start()
    copy_b.start()
    copies[0].start()
    copy_v.start()
    for c in copies[1:]:
        c.start()
    lane = lax.broadcasted_iota(jnp.int32, (1, STATE), 1)
    keep = jnp.zeros((1, STATE), f32)
    for level in range(LEVELS):
        inside = (lane >= RANK * level) & (lane < RANK * level + jnp.minimum(ranks[level], RANK))
        keep = jnp.where(inside, 1.0, keep)
    keeps[...] = jnp.broadcast_to(keep, keeps.shape)
    copy_u.wait()
    copy_b.wait()
    x[:STATE] = (u[...] * keep.astype(bf16)).T
    x[STATE:] = jnp.concatenate([b[...], jnp.zeros((8, size), bf16)], axis=0)
    for i in range(n):
        rows = slice(CHUNK * i, CHUNK * (i + 1))
        copies[i].wait()
        if i == 0:
            copy_v.wait()
        product = mul(x[...], d[rows], NT)
        rounded = product[:STATE].astype(bf16)
        mapped[:, rows] = rounded
        part = product[STATE : STATE + 8]
        base[:, rows] = part
        joined = jnp.concatenate([rounded, *thirds(part)], axis=0)
        total = mul(joined, v[rows])
        if i == 0:
            acc[...] = total
        else:
            acc[...] += total
    rhs = (acc[STATE : STATE + 8] + acc[STATE + 8 : STATE + 16] + acc[STATE + 16 :]) * keep
    places = Places(-1)
    for position in range(PIECES[0]):
        one, zero, valid = places.next_piece(position)
        m, lane_piece = places.nth(one, 1), places.nth(zero, 0)
        rows = pl.ds(pl.multiple_of(RANK * m, RANK), RANK)
        lanes = pl.ds(pl.multiple_of(2 * RANK * (lane_piece // 2), 2 * RANK), 2 * RANK)
        tile = acc[rows, lanes] * keeps[:1, lanes]
        block = jnp.where(lane_piece % 2 == 1, tile[:, RANK:], tile[:, :RANK])
        send[RANK // 2 * position : RANK // 2 * (position + 1)] = folded(jnp.where(valid, block, 0.0))
    for tile in range(LEVELS // 2):
        row = RANK // 2 * PIECES[0] + 8 * tile
        send[row : row + 8] = rhs[:, 2 * RANK * tile : 2 * RANK * (tile + 1)]


def level_kernel(level, own, got, send, left):
    places = Places(level)
    is_upper = upper(level)
    count = PIECES[level]
    rhs_row = RANK // 2 * count
    tiles = LEVELS // 2 - level // 2
    lower_of = lambda index: unfolded(
        jnp.where(is_upper, piece(got, index, count), piece(own, index, count))
    )
    upper_of = lambda index: unfolded(
        jnp.where(is_upper, piece(own, index, count), piece(got, index, count))
    )
    own_rhs = jnp.concatenate([own[rhs_row + 8 * t : rhs_row + 8 * t + 8] for t in range(tiles)], axis=1)
    got_rhs = jnp.concatenate([got[rhs_row + 8 * t : rhs_row + 8 * t + 8] for t in range(tiles)], axis=1)
    skip = RANK * (level % 2)
    pivot_rhs = jnp.where(is_upper, got_rhs, own_rhs)[:, skip : skip + RANK]
    for position in range(PIECES[level + 1]):
        one, zero, valid = places.next_piece(position)
        index = one * places.zeros + zero
        product = wide_mul(lower_of(places.inner + one), upper_of(places.inner + zero))
        block = piece(own, index, count) + piece(got, index, count) - folded(product)
        send[RANK // 2 * position : RANK // 2 * (position + 1)] = jnp.where(valid, block, 0.0)
    rights = []
    lefts = []
    for k in range(places.count):
        zeros_before = k - places.ones_before[k]
        right = upper_of(places.inner + zeros_before)
        rights.append(jnp.where(places.bits[k] == 0, right, 0.0))
        theirs = unfolded(piece(got, places.inner + places.ones_before[k], count))
        lefts.append(jnp.where(is_upper & (places.bits[k] == 1), theirs, 0.0))
    blank = jnp.zeros((RANK, RANK + skip), f32)
    product = wide_mul(pivot_rhs, jnp.concatenate([blank, *rights], axis=1))
    rhs = own_rhs + got_rhs - product
    skip_tiles = level % 2
    for t in range(skip_tiles, tiles):
        row = RANK // 2 * PIECES[level + 1] + 8 * (t - skip_tiles)
        send[row : row + 8] = rhs[:, 2 * RANK * t : 2 * RANK * (t + 1)]
    lefts.append(jnp.where(is_upper, pivot_rhs, 0.0))
    left[...] = jnp.concatenate(lefts, axis=0)


def coefficients(left, t):
    if t is None:
        return -left
    return jnp.concatenate([t[RANK:] - wide_mul(left, t[:RANK]), -left], axis=1)


def coefficient_kernel(*refs):
    t = None
    for left in refs[:-1]:
        t = coefficients(left[...], t)
    refs[-1][...] = t


def basis_kernel(left, t_ref, mapped, base, high_low, shifted):
    t = coefficients(left[...], t_ref[...])
    w = mapped[...]
    high, low = halves(t)
    rows = t.shape[0]
    product = mul(jnp.concatenate([high, low], axis=0), w[: t.shape[1]])
    product = product[:rows] + product[rows:]
    high, low = halves(w[4 * RANK :].astype(f32) + product[: 2 * RANK])
    high_low[: 2 * RANK] = high
    high_low[2 * RANK :] = low
    shifted[...] = base[...] + product[2 * RANK :]


def last_kernel(near, far, across, high_low, shifted, out):
    group = lax.axis_index("leaf") >> 4 & 3
    half = RANK // 2
    zero = jnp.where(group == 1, near[half:], jnp.where(group == 2, far[half:], across[half:]))
    one = jnp.where(group == 2, across[...], far[...])
    two = near[...]
    value_5 = zero[:, RANK:] + one[half:, RANK:] - wide_mul(zero[:, :RANK], unfolded(one[:half]))
    value_5 = jnp.where(group >= 2, value_5, 0.0)
    value_4 = two[half:, :RANK] - wide_mul(value_5, unfolded(two[:half]))
    value_4 = jnp.where(group == 3, value_4, jnp.where(group == 1, zero[:, :RANK], 0.0))
    high, low = halves(jnp.concatenate([value_4, value_5], axis=1))
    joined = jnp.concatenate(
        [jnp.concatenate([high, high], axis=1), jnp.concatenate([low, low], axis=1)], axis=0
    )
    product = mul(joined, high_low[...])
    out[...] = shifted[...] - (product[:8] + product[8:])


def send_shape(level):
    return (RANK // 2 * PIECES[level] + 8 * (LEVELS // 2 - level // 2), 2 * RANK)


def call(kernel, name, outs, *args, after=()):
    vmem = pl.BlockSpec(memory_space=pltpu.VMEM)
    count = len(args)

    def body(*refs):
        kernel(*refs[:count], *refs[count + len(after) :])

    return pl.pallas_call(
        body,
        name=name,
        in_specs=[vmem] * count + [pl.BlockSpec(memory_space=pl.ANY)] * len(after),
        out_specs=[vmem] * len(outs),
        out_shape=[jax.ShapeDtypeStruct(s, t) for s, t in outs],
        compiler_params=pltpu.CompilerParams(vmem_limit_bytes=16 << 20),
    )(*args, *after)


def swapped(x, distance):
    return lax.ppermute(x, "leaf", [(i, i ^ distance) for i in range(lax.axis_size("leaf"))])


def raised(x, distance):
    pairs = [(i, i ^ distance) for i in range(lax.axis_size("leaf"))]
    return lax.ppermute(x, "leaf", [(i, j) for i, j in pairs if i < j])


def on_device(rhs_vectors, diag_inverse, left_factors, right_factors, ranks):
    size = diag_inverse.shape[0]
    vmem = pl.BlockSpec(memory_space=pltpu.VMEM)
    hbm = pl.BlockSpec(memory_space=pltpu.HBM)
    mapped, base, send = pl.pallas_call(
        first_kernel,
        name="first",
        in_specs=[pl.BlockSpec(memory_space=pltpu.SMEM), hbm, hbm, hbm, hbm],
        out_specs=[vmem] * 3,
        out_shape=[
            jax.ShapeDtypeStruct((STATE, size), bf16),
            jax.ShapeDtypeStruct((8, size), f32),
            jax.ShapeDtypeStruct(send_shape(0), f32),
        ],
        scratch_shapes=[
            pltpu.VMEM((size, size), bf16),
            pltpu.VMEM((size, STATE), bf16),
            pltpu.VMEM((size, STATE), bf16),
            pltpu.VMEM((8, size), bf16),
            pltpu.VMEM((STATE + 16, size), bf16),
            pltpu.VMEM((STATE + 24, STATE), f32),
            pltpu.VMEM((8, STATE), f32),
            pltpu.SemaphoreType.DMA((size // CHUNK + 3,)),
        ],
        compiler_params=pltpu.CompilerParams(vmem_limit_bytes=40 << 20),
    )(
        *(
            pltpu.with_memory_space_constraint(a, pltpu.HBM)
            for a in (ranks, rhs_vectors, diag_inverse, left_factors, right_factors)
        ),
    )
    lefts = []
    for level in range(4):
        got = swapped(send, PARTNER[level])
        after = ()
        if level == 3:
            (t,) = after = call(coefficient_kernel, "coefficients", [((3 * RANK + 8, 3 * RANK), f32)], *lefts)
        send, left = call(
            lambda *refs, level=level: level_kernel(level, *refs),
            f"level_{level}",
            [(send_shape(level + 1), f32), ((RANK * (LEVELS - 1 - level) + 8, RANK), f32)],
            send,
            got,
            after=after,
        )
        lefts.append(left)
    far, across, near = raised(send, 32), raised(send, 48), raised(send, 16)
    high_low, shifted = call(
        basis_kernel, "basis", [((4 * RANK, size), bf16), ((8, size), f32)], lefts[3], t, mapped, base
    )
    (out,) = call(last_kernel, "last", [((8, size), f32)], near, far, across, high_low, shifted)
    return out


def solution(mesh):
    in_specs = (P("rhs", "leaf"), P("leaf", None), P("leaf", None), P("leaf", None), P())
    out_specs = P("rhs", "leaf")
    return jax.shard_map(
        on_device, mesh=mesh, in_specs=in_specs, out_specs=out_specs, check_vma=False
    )
```

```python
import jax
import jax.numpy as jnp
from jax import lax
from jax.experimental import pallas as pl
from jax.experimental.pallas import tpu as pltpu
from jax.sharding import PartitionSpec as P

f32 = jnp.float32
bf16 = jnp.bfloat16
NN = (((1,), (0,)), ((), ()))
NT = (((1,), (1,)), ((), ()))
RANK = 64
LEVELS = 6
STATE = RANK * LEVELS
CHUNK = 512
PARTNER = (1, 2, 4, 12, 16, 48)
PIECES = (9, 6, 4, 2, 1, 0)


def mul(a, b, dims=NN):
    return lax.dot_general(a, b, dims, preferred_element_type=f32)


def halves(x):
    high = x.astype(bf16)
    return high, (x - high.astype(f32)).astype(bf16)


def thirds(x):
    high, low = halves(x)
    rest = x - high.astype(f32) - low.astype(f32)
    return high, low, rest.astype(bf16)


def wide_mul(a, b):
    a_high, a_low = halves(a)
    b_high, b_low = halves(b)
    return mul(
        jnp.concatenate([a_high, a_high, a_low], axis=1),
        jnp.concatenate([b_high, b_low, b_high], axis=0),
    )


def upper(level):
    return (lax.axis_index("leaf") >> level & 1) == 1


def folded(x):
    return jnp.concatenate([x[: RANK // 2], x[RANK // 2 :]], axis=1)


def unfolded(x):
    return jnp.concatenate([x[:, :RANK], x[:, RANK:]], axis=0)


class Places:
    def __init__(self, level):
        self.count = LEVELS - 1 - level
        leaf = lax.axis_index("leaf")
        self.bits = [(leaf >> (level + 1 + k)) & 1 for k in range(self.count)]
        self.ones_before = [sum(self.bits[:k], jnp.int32(0)) for k in range(self.count + 1)]
        self.ones = self.ones_before[-1]
        self.zeros = self.count - self.ones
        self.inner = self.ones * self.zeros

    def next_piece(self, position):
        own = self.bits[0]
        ones, zeros = self.ones - own, self.zeros - (1 - own)
        inner = ones * zeros
        within = position < inner
        a = sum([(position >= t * zeros).astype(jnp.int32) for t in range(1, self.count)], jnp.int32(0))
        b = position - a * zeros
        rest = position - inner
        a = jnp.where(within, a + own, jnp.where(own == 1, 0, rest))
        b = jnp.where(within, b + 1 - own, jnp.where(own == 1, rest, 0))
        valid = (a < self.ones) & (b < self.zeros)
        return jnp.where(valid, a, 0), jnp.where(valid, b, 0), valid

    def nth(self, n, bit):
        found = jnp.int32(0)
        for k in range(self.count):
            before = self.ones_before[k] if bit else k - self.ones_before[k]
            found = jnp.where((before == n) & (self.bits[k] == bit), k, found)
        return found


def piece(ref, index, limit):
    index = jnp.minimum(index, limit - 1)
    return ref[pl.ds(pl.multiple_of(RANK // 2 * index, RANK // 2), RANK // 2)]


def keep_row(ranks):
    lane = lax.broadcasted_iota(jnp.int32, (8, STATE), 1)
    keep = jnp.zeros((8, STATE), f32)
    for level in range(LEVELS):
        inside = (lane >= RANK * level) & (lane < RANK * level + jnp.minimum(ranks[level], RANK))
        keep = jnp.where(inside, 1.0, keep)
    return keep


def turned_rhs(b):
    wide = b[...].astype(f32)
    gap = jnp.zeros((RANK - 8, wide.shape[1]), f32)
    return jnp.concatenate([wide, gap, wide, gap], axis=0).T.astype(bf16)


def few_ones(places, d, u, v, b, x, acc, rhs, copies, copy_u, copy_b, copy_v):
    copy_u.start()
    copy_b.start()
    copies[0].start()
    copy_v.start()
    for c in copies[1:]:
        c.start()
    tile_0, tile_1, free = tiles_of(places)
    copy_b.wait()
    extra = turned_rhs(b)
    copy_u.wait()
    lane = lax.broadcasted_iota(jnp.int32, extra.shape, 1)
    x[:, : 2 * RANK] = u[:, pl.ds(pl.multiple_of(2 * RANK * tile_0, 2 * RANK), 2 * RANK)]
    second = u[:, pl.ds(pl.multiple_of(2 * RANK * tile_1, 2 * RANK), 2 * RANK)]
    x[:, 2 * RANK :] = jnp.where(lane // RANK == free, extra, second)
    count = len(copies)

    def gather(i, joined):
        total = mul(joined, v[CHUNK * i : CHUNK * (i + 1)])
        if i == 0:
            acc[: 4 * RANK + 16] = total
        else:
            acc[: 4 * RANK + 16] += total

    joined = None
    for i in range(count):
        copies[i].wait()
        if i == 1:
            copy_v.wait()
        middle = CHUNK * i + CHUNK // 2
        ahead = [
            mul(d[CHUNK * i : middle], x[...]),
            mul(d[middle : CHUNK * (i + 1)], x[...]),
        ]
        if i > 0:
            gather(i - 1, joined)
        product = jnp.concatenate(ahead, axis=0)
        base = product[:, 2 * RANK :].T
        base = jnp.where(free == 1, base[RANK : RANK + 8], base[:8])
        _, low, rest = thirds(base)
        joined = jnp.concatenate([product.astype(bf16).T, low, rest], axis=0)
    gather(count - 1, joined)
    start = pl.multiple_of(2 * RANK + RANK * free, RANK)
    rhs[...] = acc[pl.ds(start, 8)] + acc[4 * RANK : 4 * RANK + 8] + acc[4 * RANK + 8 : 4 * RANK + 16]


def few_zeros(places, d, u, v, b, turned, z, acc, rhs, copies, copy_u, copy_b, copy_v):
    copy_v.start()
    copies[0].start()
    copy_b.start()
    for c in copies[1:]:
        c.start()
    copy_u.start()
    zeros = [places.nth(n, 0) for n in range(3)]
    copy_v.wait()
    for i, c in enumerate(copies):
        c.wait()
        part = slice(CHUNK * i, CHUNK * (i + 1))
        turned[...] = v[part].T
        rows = [turned[pl.ds(pl.multiple_of(RANK * n, RANK), RANK)] for n in zeros]
        product = mul(jnp.concatenate(rows, axis=0), d[part])
        if i == 0:
            z[...] = product
        else:
            z[...] += product
    copy_b.wait()
    copy_u.wait()
    high, low = halves(z[...])
    both = jnp.concatenate([high, low], axis=0)
    product = mul(both, u[...])
    product = product[: 3 * RANK] + product[3 * RANK :]
    product = jnp.concatenate([product, jnp.zeros((RANK, STATE), f32)], axis=0)
    acc[:STATE, : 4 * RANK] = product.T
    twice = jnp.concatenate([b[...], b[...]], axis=0)
    shares = mul(twice, both, NT)[:8]
    shares = shares[:, : 3 * RANK] + shares[:, 3 * RANK :]
    pieces = []
    for k in range(LEVELS):
        before = k - places.ones_before[k]
        chosen = jnp.where(before == 1, shares[:, RANK : 2 * RANK], shares[:, :RANK])
        pieces.append(jnp.where(before == 2, shares[:, 2 * RANK :], chosen))
    rhs[...] = jnp.concatenate(pieces, axis=1)


def tiles_of(places):
    one_0, one_1 = places.nth(0, 1), places.nth(1, 1)
    one_0 = jnp.where(places.ones > 0, one_0, 0)
    one_1 = jnp.where(places.ones > 1, one_1, one_0)
    tile_0, tile_1 = one_0 // 2, one_1 // 2
    apart = tile_1 != tile_0
    free = jnp.where(apart, 1 - one_1 % 2, 0)
    tile_1 = jnp.where(apart, tile_1, (tile_0 + 1) % (LEVELS // 2))
    return tile_0, tile_1, free


def first_kernel(ranks, b_hbm, d_hbm, u_hbm, v_hbm, send, d, u, b, keeps, v, x, turned, z, acc, rhs, sems):
    n = d.shape[0] // CHUNK
    copies = [
        pltpu.make_async_copy(d_hbm.at[pl.ds(CHUNK * i, CHUNK)], d.at[pl.ds(CHUNK * i, CHUNK)], sems.at[i])
        for i in range(n)
    ]
    copy_u = pltpu.make_async_copy(u_hbm, u, sems.at[n])
    copy_b = pltpu.make_async_copy(b_hbm, b, sems.at[n + 1])
    copy_v = pltpu.make_async_copy(v_hbm, v, sems.at[n + 2])
    places = Places(-1)
    few = places.ones <= 2

    @pl.when(few)
    def _():
        few_ones(places, d, u, v, b, x, acc, rhs, copies, copy_u, copy_b, copy_v)

    @pl.when(jnp.logical_not(few))
    def _():
        few_zeros(places, d, u, v, b, turned, z, acc, rhs, copies, copy_u, copy_b, copy_v)

    keeps[...] = keep_row(ranks)
    tile_0, _, _ = tiles_of(places)
    row_id = lax.broadcasted_iota(jnp.int32, (RANK, RANK), 0)
    lane_id = lax.broadcasted_iota(jnp.int32, (RANK, RANK), 1)
    for position in range(PIECES[0]):
        one, zero, valid = places.next_piece(position)
        m, l = places.nth(one, 1), places.nth(zero, 0)
        start = jnp.where(few, jnp.where(m // 2 == tile_0, 0, 2 * RANK) + RANK * (m % 2), RANK * m)
        lane_piece = jnp.where(few, l, jnp.minimum(zero, 2))
        rows = pl.ds(pl.multiple_of(start, RANK), RANK)
        lanes = pl.ds(pl.multiple_of(2 * RANK * (lane_piece // 2), 2 * RANK), 2 * RANK)
        tile = acc[rows, lanes]
        block = jnp.where(lane_piece % 2 == 1, tile[:, RANK:], tile[:, :RANK])
        used = (row_id < ranks[m]) & (lane_id < jnp.where(valid, ranks[l], 0))
        send[RANK // 2 * position : RANK // 2 * (position + 1)] = folded(jnp.where(used, block, 0.0))
    kept = rhs[...] * keeps[...]
    for tile in range(LEVELS // 2):
        row = RANK // 2 * PIECES[0] + 8 * tile
        send[row : row + 8] = kept[:, 2 * RANK * tile : 2 * RANK * (tile + 1)]


def mapped_kernel(half, d, u, b, keeps, mapped, base):
    size = d.shape[0] // 2
    joined = jnp.concatenate([u[...], turned_rhs(b)], axis=1)
    for i in range(size // CHUNK):
        part = slice(CHUNK * i, CHUNK * (i + 1))
        product = mul(d[size * half + CHUNK * i : size * half + CHUNK * (i + 1)], joined)
        mapped[:, part] = (product[:, :STATE] * keeps[:1]).astype(bf16).T
        base[:, part] = product[:, STATE:].T[:8]


def level_kernel(level, own, got, send, left):
    places = Places(level)
    is_upper = upper(level)
    count = PIECES[level]
    rhs_row = RANK // 2 * count
    tiles = LEVELS // 2 - level // 2
    lower_of = lambda index: unfolded(
        jnp.where(is_upper, piece(got, index, count), piece(own, index, count))
    )
    upper_of = lambda index: unfolded(
        jnp.where(is_upper, piece(own, index, count), piece(got, index, count))
    )
    own_rhs = jnp.concatenate([own[rhs_row + 8 * t : rhs_row + 8 * t + 8] for t in range(tiles)], axis=1)
    got_rhs = jnp.concatenate([got[rhs_row + 8 * t : rhs_row + 8 * t + 8] for t in range(tiles)], axis=1)
    skip = RANK * (level % 2)
    pivot_rhs = jnp.where(is_upper, got_rhs, own_rhs)[:, skip : skip + RANK]
    for position in range(PIECES[level + 1]):
        one, zero, valid = places.next_piece(position)
        index = one * places.zeros + zero
        product = wide_mul(lower_of(places.inner + one), upper_of(places.inner + zero))
        block = piece(own, index, count) + piece(got, index, count) - folded(product)
        send[RANK // 2 * position : RANK // 2 * (position + 1)] = jnp.where(valid, block, 0.0)
    rights = []
    lefts = []
    for k in range(places.count):
        zeros_before = k - places.ones_before[k]
        right = upper_of(places.inner + zeros_before)
        rights.append(jnp.where(places.bits[k] == 0, right, 0.0))
        theirs = unfolded(piece(got, places.inner + places.ones_before[k], count))
        lefts.append(jnp.where(is_upper & (places.bits[k] == 1), theirs, 0.0))
    blank = jnp.zeros((RANK, RANK + skip), f32)
    product = wide_mul(pivot_rhs, jnp.concatenate([blank, *rights], axis=1))
    rhs = own_rhs + got_rhs - product
    skip_tiles = level % 2
    for t in range(skip_tiles, tiles):
        row = RANK // 2 * PIECES[level + 1] + 8 * (t - skip_tiles)
        send[row : row + 8] = rhs[:, 2 * RANK * t : 2 * RANK * (t + 1)]
    lefts.append(jnp.where(is_upper, pivot_rhs, 0.0))
    left[...] = jnp.concatenate(lefts, axis=0)


def coefficients(left, t):
    if t is None:
        return -left
    return jnp.concatenate([t[RANK:] - wide_mul(left, t[:RANK]), -left], axis=1)


def coefficient_kernel(*refs):
    t = None
    for left in refs[:-1]:
        t = coefficients(left[...], t)
    refs[-1][...] = t


def basis_kernel(left, t_ref, mapped_0, mapped_1, base_0, base_1, out):
    t = coefficients(left[...], t_ref[...])
    w = jnp.concatenate([mapped_0[...], mapped_1[...]], axis=1)
    high, low = halves(t)
    rows = t.shape[0]
    product = mul(jnp.concatenate([high, low], axis=0), w[: t.shape[1]])
    product = product[:rows] + product[rows:]
    out[: 2 * RANK] = w[4 * RANK :].astype(f32) + product[: 2 * RANK]
    base = jnp.concatenate([base_0[...], base_1[...]], axis=1)
    out[2 * RANK :] = base + product[2 * RANK :]


def late_kernel(left, basis, high_low, shifted):
    update = basis[RANK:] - wide_mul(left[...], basis[:RANK])
    high, low = halves(update[:RANK])
    high_low[:RANK] = high
    high_low[RANK : 2 * RANK] = low
    high_low[2 * RANK :] = high
    shifted[...] = update[RANK:]


def last_kernel(got, high_low, shifted, out):
    value = jnp.where(upper(5), got[:, RANK:], 0.0)
    high, low = halves(value)
    out[...] = shifted[...] - mul(jnp.concatenate([high, high, low], axis=1), high_low[...])


def send_shape(level):
    return (RANK // 2 * PIECES[level] + 8 * (LEVELS // 2 - level // 2), 2 * RANK)


def call(kernel, name, outs, *args, after=()):
    vmem = pl.BlockSpec(memory_space=pltpu.VMEM)
    count = len(args)

    def body(*refs):
        kernel(*refs[:count], *refs[count + len(after) :])

    return pl.pallas_call(
        body,
        name=name,
        in_specs=[vmem] * count + [pl.BlockSpec(memory_space=pl.ANY)] * len(after),
        out_specs=[vmem] * len(outs),
        out_shape=[jax.ShapeDtypeStruct(s, t) for s, t in outs],
        compiler_params=pltpu.CompilerParams(vmem_limit_bytes=16 << 20),
    )(*args, *after)


def swapped(x, distance):
    return lax.ppermute(x, "leaf", [(i, i ^ distance) for i in range(lax.axis_size("leaf"))])


def on_device(rhs_vectors, diag_inverse, left_factors, right_factors, ranks):
    size = diag_inverse.shape[0]
    vmem = pl.BlockSpec(memory_space=pltpu.VMEM)
    hbm = pl.BlockSpec(memory_space=pltpu.HBM)
    send, d, u, b, keeps = pl.pallas_call(
        first_kernel,
        name="first",
        in_specs=[pl.BlockSpec(memory_space=pltpu.SMEM), hbm, hbm, hbm, hbm],
        out_specs=[vmem] * 5,
        out_shape=[
            jax.ShapeDtypeStruct(send_shape(0), f32),
            jax.ShapeDtypeStruct((size, size), bf16),
            jax.ShapeDtypeStruct((size, STATE), bf16),
            jax.ShapeDtypeStruct((8, size), bf16),
            jax.ShapeDtypeStruct((8, STATE), f32),
        ],
        scratch_shapes=[
            pltpu.VMEM((size, STATE), bf16),
            pltpu.VMEM((size, 4 * RANK), bf16),
            pltpu.VMEM((STATE, CHUNK), bf16),
            pltpu.VMEM((3 * RANK, size), f32),
            pltpu.VMEM((STATE, STATE), f32),
            pltpu.VMEM((8, STATE), f32),
            pltpu.SemaphoreType.DMA((size // CHUNK + 3,)),
        ],
        compiler_params=pltpu.CompilerParams(vmem_limit_bytes=30 << 20),
    )(
        *(
            pltpu.with_memory_space_constraint(a, pltpu.HBM)
            for a in (ranks, rhs_vectors, diag_inverse, left_factors, right_factors)
        ),
    )
    mapped = []
    lefts = []
    basis = t = None
    for level in range(LEVELS - 1):
        got = swapped(send, PARTNER[level])
        after = ()
        if level in (1, 2):
            after = call(
                lambda *refs, half=level - 1: mapped_kernel(half, *refs),
                f"mapped_{level}",
                [((STATE, size // 2), bf16), ((8, size // 2), f32)],
                d,
                u,
                b,
                keeps,
                after=(send,),
            )
            mapped.append(after)
        if level == 3:
            (t,) = after = call(coefficient_kernel, "coefficients", [((3 * RANK + 8, 3 * RANK), f32)], *lefts)
        if level == 4:
            (basis,) = after = call(
                basis_kernel, "basis", [((2 * RANK + 8, size), f32)], lefts[3], t, *(m[0] for m in mapped), *(m[1] for m in mapped)
            )
        send, left = call(
            lambda *refs, level=level: level_kernel(level, *refs),
            f"level_{level}",
            [(send_shape(level + 1), f32), ((RANK * (LEVELS - 1 - level) + 8, RANK), f32)],
            send,
            got,
            after=after,
        )
        lefts.append(left)
    got = swapped(send, PARTNER[LEVELS - 1])
    high_low, shifted = call(
        late_kernel, "late", [((3 * RANK, size), bf16), ((8, size), f32)], lefts[4], basis
    )
    (out,) = call(last_kernel, "last", [((8, size), f32)], got, high_low, shifted)
    return out


def solution(mesh):
    in_specs = (P("rhs", "leaf"), P("leaf", None), P("leaf", None), P("leaf", None), P())
    out_specs = P("rhs", "leaf")
    return jax.shard_map(
        on_device, mesh=mesh, in_specs=in_specs, out_specs=out_specs, check_vma=False
    )
```

```python
import jax
import jax.numpy as jnp
from jax import lax
from jax.experimental import pallas as pl
from jax.experimental.pallas import tpu as pltpu
from jax.sharding import PartitionSpec as P

f32 = jnp.float32
bf16 = jnp.bfloat16
NN = (((1,), (0,)), ((), ()))
NT = (((1,), (1,)), ((), ()))
RANK = 64
LEVELS = 6
STATE = RANK * LEVELS
CHUNK = 512
FEW_CHUNKS = (512, 768, 768)
MANY_CHUNKS = (256, 256, 512, 512, 512)
PARTNER = (1, 2, 4, 12, 16, 48)
PIECES = (9, 6, 4, 2, 1, 0)


def mul(a, b, dims=NN):
    return lax.dot_general(a, b, dims, preferred_element_type=f32)


def halves(x):
    high = x.astype(bf16)
    return high, (x - high.astype(f32)).astype(bf16)


def thirds(x):
    high, low = halves(x)
    rest = x - high.astype(f32) - low.astype(f32)
    return high, low, rest.astype(bf16)


def wide_mul(a, b):
    a_high, a_low = halves(a)
    b_high, b_low = halves(b)
    return mul(
        jnp.concatenate([a_high, a_high, a_low], axis=1),
        jnp.concatenate([b_high, b_low, b_high], axis=0),
    )


def upper(level):
    return (lax.axis_index("leaf") >> level & 1) == 1


def folded(x):
    return jnp.concatenate([x[: RANK // 2], x[RANK // 2 :]], axis=1)


def unfolded(x):
    return jnp.concatenate([x[:, :RANK], x[:, RANK:]], axis=0)


class Places:
    def __init__(self, level):
        self.count = LEVELS - 1 - level
        leaf = lax.axis_index("leaf")
        self.bits = [(leaf >> (level + 1 + k)) & 1 for k in range(self.count)]
        self.ones_before = [sum(self.bits[:k], jnp.int32(0)) for k in range(self.count + 1)]
        self.ones = self.ones_before[-1]
        self.zeros = self.count - self.ones
        self.inner = self.ones * self.zeros

    def next_piece(self, position):
        own = self.bits[0]
        ones, zeros = self.ones - own, self.zeros - (1 - own)
        inner = ones * zeros
        within = position < inner
        a = sum([(position >= t * zeros).astype(jnp.int32) for t in range(1, self.count)], jnp.int32(0))
        b = position - a * zeros
        rest = position - inner
        a = jnp.where(within, a + own, jnp.where(own == 1, 0, rest))
        b = jnp.where(within, b + 1 - own, jnp.where(own == 1, rest, 0))
        valid = (a < self.ones) & (b < self.zeros)
        return jnp.where(valid, a, 0), jnp.where(valid, b, 0), valid

    def nth(self, n, bit):
        found = jnp.int32(0)
        for k in range(self.count):
            before = self.ones_before[k] if bit else k - self.ones_before[k]
            found = jnp.where((before == n) & (self.bits[k] == bit), k, found)
        return found


def piece(ref, index, limit):
    index = jnp.minimum(index, limit - 1)
    return ref[pl.ds(pl.multiple_of(RANK // 2 * index, RANK // 2), RANK // 2)]


def keep_row(ranks):
    lane = lax.broadcasted_iota(jnp.int32, (8, STATE), 1)
    keep = jnp.zeros((8, STATE), f32)
    for level in range(LEVELS):
        inside = (lane >= RANK * level) & (lane < RANK * level + jnp.minimum(ranks[level], RANK))
        keep = jnp.where(inside, 1.0, keep)
    return keep


def turned_rhs(b):
    wide = b[...].astype(f32)
    gap = jnp.zeros((RANK - 8, wide.shape[1]), f32)
    return jnp.concatenate([wide, gap, wide, gap], axis=0).T.astype(bf16)


def few_ones(places, d, u, v, b, x, acc, rhs, copies, copy_u, copy_b, copy_v):
    tile_0, tile_1, free = tiles_of(places)
    copy_b.wait()
    extra = turned_rhs(b)
    copy_u.wait()
    lane = lax.broadcasted_iota(jnp.int32, extra.shape, 1)
    x[:, : 2 * RANK] = u[:, pl.ds(pl.multiple_of(2 * RANK * tile_0, 2 * RANK), 2 * RANK)]
    second = u[:, pl.ds(pl.multiple_of(2 * RANK * tile_1, 2 * RANK), 2 * RANK)]
    x[:, 2 * RANK :] = jnp.where(lane // RANK == free, extra, second)
    count = len(copies)
    starts = [sum(FEW_CHUNKS[:i]) for i in range(count + 1)]

    def gather(i, joined):
        total = mul(joined, v[starts[i] : starts[i + 1]])
        if i == 0:
            acc[: 4 * RANK + 16] = total
        else:
            acc[: 4 * RANK + 16] += total

    joined = None
    for i in range(count):
        copies[i].wait()
        if i == 1:
            copy_v.wait()
        middle = (starts[i] + starts[i + 1]) // 2
        ahead = [mul(d[starts[i] : middle], x[...]), mul(d[middle : starts[i + 1]], x[...])]
        if i > 0:
            gather(i - 1, joined)
        product = jnp.concatenate(ahead, axis=0)
        base = product[:, 2 * RANK :].T
        base = jnp.where(free == 1, base[RANK : RANK + 8], base[:8])
        _, low, rest = thirds(base)
        joined = jnp.concatenate([product.astype(bf16).T, low, rest], axis=0)
    gather(count - 1, joined)
    start = pl.multiple_of(2 * RANK + RANK * free, RANK)
    rhs[...] = acc[pl.ds(start, 8)] + acc[4 * RANK : 4 * RANK + 8] + acc[4 * RANK + 8 : 4 * RANK + 16]


def few_zeros(places, d, u, v, b, turned, z, acc, rhs, copies, copy_u, copy_b, copy_v):
    zeros = [places.nth(n, 0) for n in range(3)]
    starts = [sum(MANY_CHUNKS[:i]) for i in range(len(copies) + 1)]

    def turn(i):
        turned[:, starts[i] : starts[i + 1]] = v[starts[i] : starts[i + 1]].T

    copy_v.wait()
    turn(0)
    for i, c in enumerate(copies):
        c.wait()
        part = slice(starts[i], starts[i + 1])
        rows = [turned[pl.ds(pl.multiple_of(RANK * n, RANK), RANK), part] for n in zeros]
        product = mul(jnp.concatenate(rows, axis=0), d[part])
        if i + 1 < len(copies):
            turn(i + 1)
        if i == 0:
            z[...] = product
        else:
            z[...] += product
    copy_b.wait()
    copy_u.wait()
    high, low = halves(z[...])
    both = jnp.concatenate([high, low], axis=0)
    product = mul(both, u[...])
    product = product[: 3 * RANK] + product[3 * RANK :]
    product = jnp.concatenate([product, jnp.zeros((RANK, STATE), f32)], axis=0)
    acc[:STATE, : 4 * RANK] = product.T
    twice = jnp.concatenate([b[...], b[...]], axis=0)
    shares = mul(twice, both, NT)[:8]
    shares = shares[:, : 3 * RANK] + shares[:, 3 * RANK :]
    pieces = []
    for k in range(LEVELS):
        before = k - places.ones_before[k]
        chosen = jnp.where(before == 1, shares[:, RANK : 2 * RANK], shares[:, :RANK])
        pieces.append(jnp.where(before == 2, shares[:, 2 * RANK :], chosen))
    rhs[...] = jnp.concatenate(pieces, axis=1)


def tiles_of(places):
    one_0, one_1 = places.nth(0, 1), places.nth(1, 1)
    one_0 = jnp.where(places.ones > 0, one_0, 0)
    one_1 = jnp.where(places.ones > 1, one_1, one_0)
    tile_0, tile_1 = one_0 // 2, one_1 // 2
    apart = tile_1 != tile_0
    free = jnp.where(apart, 1 - one_1 % 2, 0)
    tile_1 = jnp.where(apart, tile_1, (tile_0 + 1) % (LEVELS // 2))
    return tile_0, tile_1, free


def first_kernel(ranks, b_hbm, d_hbm, u_hbm, v_hbm, send, d, u, b, keeps, v, x, turned, z, acc, rhs, sems):
    n = max(len(FEW_CHUNKS), len(MANY_CHUNKS))

    def pieces_of(sizes):
        parts = [pl.ds(sum(sizes[:i]), sizes[i]) for i in range(len(sizes))]
        return [pltpu.make_async_copy(d_hbm.at[p], d.at[p], sems.at[i]) for i, p in enumerate(parts)]

    copy_u = pltpu.make_async_copy(u_hbm, u, sems.at[n])
    copy_b = pltpu.make_async_copy(b_hbm, b, sems.at[n + 1])
    copy_v = pltpu.make_async_copy(v_hbm, v, sems.at[n + 2])
    places = Places(-1)
    few = places.ones <= 2

    @pl.when(few)
    def _():
        copies = pieces_of(FEW_CHUNKS)
        for c in (copy_b, copy_u, copies[0], copy_v, *copies[1:]):
            c.start()

    @pl.when(jnp.logical_not(few))
    def _():
        copies = pieces_of(MANY_CHUNKS)
        for c in (copy_v, *copies, copy_u, copy_b):
            c.start()

    tile_0, _, _ = tiles_of(places)
    plan = []
    for position in range(PIECES[0]):
        one, zero, valid = places.next_piece(position)
        m, l = places.nth(one, 1), places.nth(zero, 0)
        start = jnp.where(few, jnp.where(m // 2 == tile_0, 0, 2 * RANK) + RANK * (m % 2), RANK * m)
        lane_piece = jnp.where(few, l, jnp.minimum(zero, 2))
        plan.append((start, lane_piece, ranks[m], jnp.where(valid, ranks[l], 0)))
    keeps[...] = keep_row(ranks)

    @pl.when(few)
    def _():
        few_ones(places, d, u, v, b, x, acc, rhs, pieces_of(FEW_CHUNKS), copy_u, copy_b, copy_v)

    @pl.when(jnp.logical_not(few))
    def _():
        few_zeros(places, d, u, v, b, turned, z, acc, rhs, pieces_of(MANY_CHUNKS), copy_u, copy_b, copy_v)

    row_id = lax.broadcasted_iota(jnp.int32, (RANK, RANK), 0)
    lane_id = lax.broadcasted_iota(jnp.int32, (RANK, RANK), 1)
    for position, (start, lane_piece, rank_m, rank_l) in enumerate(plan):
        rows = pl.ds(pl.multiple_of(start, RANK), RANK)
        lanes = pl.ds(pl.multiple_of(2 * RANK * (lane_piece // 2), 2 * RANK), 2 * RANK)
        tile = acc[rows, lanes]
        block = jnp.where(lane_piece % 2 == 1, tile[:, RANK:], tile[:, :RANK])
        used = (row_id < rank_m) & (lane_id < rank_l)
        send[RANK // 2 * position : RANK // 2 * (position + 1)] = folded(jnp.where(used, block, 0.0))
    kept = rhs[...] * keeps[...]
    for tile in range(LEVELS // 2):
        row = RANK // 2 * PIECES[0] + 8 * tile
        send[row : row + 8] = kept[:, 2 * RANK * tile : 2 * RANK * (tile + 1)]


def mapped_kernel(half, d, u, b, keeps, mapped, base):
    size = d.shape[0] // 2
    joined = jnp.concatenate([u[...], turned_rhs(b)], axis=1)
    for i in range(size // CHUNK):
        part = slice(CHUNK * i, CHUNK * (i + 1))
        product = mul(d[size * half + CHUNK * i : size * half + CHUNK * (i + 1)], joined)
        mapped[:, part] = (product[:, :STATE] * keeps[:1]).astype(bf16).T
        base[:, part] = product[:, STATE:].T[:8]


def level_kernel(level, own, got, send, left):
    places = Places(level)
    is_upper = upper(level)
    count = PIECES[level]
    rhs_row = RANK // 2 * count
    tiles = LEVELS // 2 - level // 2
    lower_of = lambda index: unfolded(
        jnp.where(is_upper, piece(got, index, count), piece(own, index, count))
    )
    upper_of = lambda index: unfolded(
        jnp.where(is_upper, piece(own, index, count), piece(got, index, count))
    )
    own_rhs = jnp.concatenate([own[rhs_row + 8 * t : rhs_row + 8 * t + 8] for t in range(tiles)], axis=1)
    got_rhs = jnp.concatenate([got[rhs_row + 8 * t : rhs_row + 8 * t + 8] for t in range(tiles)], axis=1)
    skip = RANK * (level % 2)
    pivot_rhs = jnp.where(is_upper, got_rhs, own_rhs)[:, skip : skip + RANK]
    for position in range(PIECES[level + 1]):
        one, zero, valid = places.next_piece(position)
        index = one * places.zeros + zero
        product = wide_mul(lower_of(places.inner + one), upper_of(places.inner + zero))
        block = piece(own, index, count) + piece(got, index, count) - folded(product)
        send[RANK // 2 * position : RANK // 2 * (position + 1)] = jnp.where(valid, block, 0.0)
    rights = []
    lefts = []
    for k in range(places.count):
        zeros_before = k - places.ones_before[k]
        right = upper_of(places.inner + zeros_before)
        rights.append(jnp.where(places.bits[k] == 0, right, 0.0))
        theirs = unfolded(piece(got, places.inner + places.ones_before[k], count))
        lefts.append(jnp.where(is_upper & (places.bits[k] == 1), theirs, 0.0))
    blank = jnp.zeros((RANK, RANK + skip), f32)
    product = wide_mul(pivot_rhs, jnp.concatenate([blank, *rights], axis=1))
    rhs = own_rhs + got_rhs - product
    skip_tiles = level % 2
    for t in range(skip_tiles, tiles):
        row = RANK // 2 * PIECES[level + 1] + 8 * (t - skip_tiles)
        send[row : row + 8] = rhs[:, 2 * RANK * t : 2 * RANK * (t + 1)]
    lefts.append(jnp.where(is_upper, pivot_rhs, 0.0))
    left[...] = jnp.concatenate(lefts, axis=0)


def coefficients(left, t):
    if t is None:
        return -left
    return jnp.concatenate([t[RANK:] - wide_mul(left, t[:RANK]), -left], axis=1)


def coefficient_kernel(*refs):
    t = None
    for left in refs[:-1]:
        t = coefficients(left[...], t)
    refs[-1][...] = t


def basis_kernel(left, t_ref, mapped_0, mapped_1, base_0, base_1, out):
    t = coefficients(left[...], t_ref[...])
    w = jnp.concatenate([mapped_0[...], mapped_1[...]], axis=1)
    high, low = halves(t)
    rows = t.shape[0]
    product = mul(jnp.concatenate([high, low], axis=0), w[: t.shape[1]])
    product = product[:rows] + product[rows:]
    out[: 2 * RANK] = w[4 * RANK :].astype(f32) + product[: 2 * RANK]
    base = jnp.concatenate([base_0[...], base_1[...]], axis=1)
    out[2 * RANK :] = base + product[2 * RANK :]


def late_kernel(left, basis, high_low, shifted):
    update = basis[RANK:] - wide_mul(left[...], basis[:RANK])
    high, low = halves(update[:RANK])
    high_low[:RANK] = high
    high_low[RANK : 2 * RANK] = low
    high_low[2 * RANK :] = high
    shifted[...] = update[RANK:]


def last_kernel(got, high_low, shifted, out):
    value = jnp.where(upper(5), got[:, RANK:], 0.0)
    high, low = halves(value)
    out[...] = shifted[...] - mul(jnp.concatenate([high, high, low], axis=1), high_low[...])


def send_shape(level):
    return (RANK // 2 * PIECES[level] + 8 * (LEVELS // 2 - level // 2), 2 * RANK)


def call(kernel, name, outs, *args, after=()):
    vmem = pl.BlockSpec(memory_space=pltpu.VMEM)
    count = len(args)

    def body(*refs):
        kernel(*refs[:count], *refs[count + len(after) :])

    return pl.pallas_call(
        body,
        name=name,
        in_specs=[vmem] * count + [pl.BlockSpec(memory_space=pl.ANY)] * len(after),
        out_specs=[vmem] * len(outs),
        out_shape=[jax.ShapeDtypeStruct(s, t) for s, t in outs],
        compiler_params=pltpu.CompilerParams(vmem_limit_bytes=16 << 20),
    )(*args, *after)


def swapped(x, distance):
    return lax.ppermute(x, "leaf", [(i, i ^ distance) for i in range(lax.axis_size("leaf"))])


def on_device(rhs_vectors, diag_inverse, left_factors, right_factors, ranks):
    size = diag_inverse.shape[0]
    vmem = pl.BlockSpec(memory_space=pltpu.VMEM)
    hbm = pl.BlockSpec(memory_space=pltpu.HBM)
    send, d, u, b, keeps = pl.pallas_call(
        first_kernel,
        name="first",
        in_specs=[pl.BlockSpec(memory_space=pltpu.SMEM), hbm, hbm, hbm, hbm],
        out_specs=[vmem] * 5,
        out_shape=[
            jax.ShapeDtypeStruct(send_shape(0), f32),
            jax.ShapeDtypeStruct((size, size), bf16),
            jax.ShapeDtypeStruct((size, STATE), bf16),
            jax.ShapeDtypeStruct((8, size), bf16),
            jax.ShapeDtypeStruct((8, STATE), f32),
        ],
        scratch_shapes=[
            pltpu.VMEM((size, STATE), bf16),
            pltpu.VMEM((size, 4 * RANK), bf16),
            pltpu.VMEM((STATE, size), bf16),
            pltpu.VMEM((3 * RANK, size), f32),
            pltpu.VMEM((STATE, STATE), f32),
            pltpu.VMEM((8, STATE), f32),
            pltpu.SemaphoreType.DMA((max(len(FEW_CHUNKS), len(MANY_CHUNKS)) + 3,)),
        ],
        compiler_params=pltpu.CompilerParams(vmem_limit_bytes=30 << 20),
    )(
        *(
            pltpu.with_memory_space_constraint(a, pltpu.HBM)
            for a in (ranks, rhs_vectors, diag_inverse, left_factors, right_factors)
        ),
    )
    mapped = []
    lefts = []
    basis = t = None
    for level in range(LEVELS - 1):
        got = swapped(send, PARTNER[level])
        after = ()
        if level in (1, 2):
            after = call(
                lambda *refs, half=level - 1: mapped_kernel(half, *refs),
                f"mapped_{level}",
                [((STATE, size // 2), bf16), ((8, size // 2), f32)],
                d,
                u,
                b,
                keeps,
                after=(send,),
            )
            mapped.append(after)
        if level == 3:
            (t,) = after = call(coefficient_kernel, "coefficients", [((3 * RANK + 8, 3 * RANK), f32)], *lefts)
        if level == 4:
            (basis,) = after = call(
                basis_kernel, "basis", [((2 * RANK + 8, size), f32)], lefts[3], t, *(m[0] for m in mapped), *(m[1] for m in mapped)
            )
        send, left = call(
            lambda *refs, level=level: level_kernel(level, *refs),
            f"level_{level}",
            [(send_shape(level + 1), f32), ((RANK * (LEVELS - 1 - level) + 8, RANK), f32)],
            send,
            got,
            after=after,
        )
        lefts.append(left)
    got = swapped(send, PARTNER[LEVELS - 1])
    high_low, shifted = call(
        late_kernel, "late", [((3 * RANK, size), bf16), ((8, size), f32)], lefts[4], basis
    )
    (out,) = call(last_kernel, "last", [((8, size), f32)], got, high_low, shifted)
    return out


def solution(mesh):
    in_specs = (P("rhs", "leaf"), P("leaf", None), P("leaf", None), P("leaf", None), P())
    out_specs = P("rhs", "leaf")
    return jax.shard_map(
        on_device, mesh=mesh, in_specs=in_specs, out_specs=out_specs, check_vma=False
    )
```

```python
import jax
import jax.numpy as jnp
from jax import lax
from jax.experimental import pallas as pl
from jax.experimental.pallas import tpu as pltpu
from jax.sharding import PartitionSpec as P

f32 = jnp.float32
bf16 = jnp.bfloat16
NN = (((1,), (0,)), ((), ()))
NT = (((1,), (1,)), ((), ()))
RANK = 64
LEVELS = 6
STATE = RANK * LEVELS
CHUNK = 512
FEW_CHUNKS = (512, 512, 512, 512)
MANY_CHUNKS = (256, 256, 512, 512, 512)
PARTNER = (1, 2, 4, 12, 16, 48)
PIECES = (9, 6, 4, 2, 1, 0)


def mul(a, b, dims=NN):
    return lax.dot_general(a, b, dims, preferred_element_type=f32)


def halves(x):
    high = x.astype(bf16)
    return high, (x - high.astype(f32)).astype(bf16)


def thirds(x):
    high, low = halves(x)
    rest = x - high.astype(f32) - low.astype(f32)
    return high, low, rest.astype(bf16)


def wide_mul(a, b):
    a_high, a_low = halves(a)
    b_high, b_low = halves(b)
    return mul(
        jnp.concatenate([a_high, a_high, a_low], axis=1),
        jnp.concatenate([b_high, b_low, b_high], axis=0),
    )


def upper(level):
    return (lax.axis_index("leaf") >> level & 1) == 1


def folded(x):
    return jnp.concatenate([x[: RANK // 2], x[RANK // 2 :]], axis=1)


def unfolded(x):
    return jnp.concatenate([x[:, :RANK], x[:, RANK:]], axis=0)


class Places:
    def __init__(self, level):
        self.count = LEVELS - 1 - level
        leaf = lax.axis_index("leaf")
        self.bits = [(leaf >> (level + 1 + k)) & 1 for k in range(self.count)]
        self.ones_before = [sum(self.bits[:k], jnp.int32(0)) for k in range(self.count + 1)]
        self.ones = self.ones_before[-1]
        self.zeros = self.count - self.ones
        self.inner = self.ones * self.zeros

    def next_piece(self, position):
        own = self.bits[0]
        ones, zeros = self.ones - own, self.zeros - (1 - own)
        inner = ones * zeros
        within = position < inner
        a = sum([(position >= t * zeros).astype(jnp.int32) for t in range(1, self.count)], jnp.int32(0))
        b = position - a * zeros
        rest = position - inner
        a = jnp.where(within, a + own, jnp.where(own == 1, 0, rest))
        b = jnp.where(within, b + 1 - own, jnp.where(own == 1, rest, 0))
        valid = (a < self.ones) & (b < self.zeros)
        return jnp.where(valid, a, 0), jnp.where(valid, b, 0), valid

    def nth(self, n, bit):
        found = jnp.int32(0)
        for k in range(self.count):
            before = self.ones_before[k] if bit else k - self.ones_before[k]
            found = jnp.where((before == n) & (self.bits[k] == bit), k, found)
        return found


def piece(ref, index, limit):
    index = jnp.minimum(index, limit - 1)
    return ref[pl.ds(pl.multiple_of(RANK // 2 * index, RANK // 2), RANK // 2)]


def keep_row(ranks):
    lane = lax.broadcasted_iota(jnp.int32, (8, STATE), 1)
    keep = jnp.zeros((8, STATE), f32)
    for level in range(LEVELS):
        inside = (lane >= RANK * level) & (lane < RANK * level + jnp.minimum(ranks[level], RANK))
        keep = jnp.where(inside, 1.0, keep)
    return keep


def turned_rhs(b):
    wide = b[...].astype(f32)
    gap = jnp.zeros((RANK - 8, wide.shape[1]), f32)
    return jnp.concatenate([wide, gap, wide, gap], axis=0).T.astype(bf16)


def few_ones(places, d, u, v, b, x, acc, rhs, copies, copies_u, copy_b, copy_v):
    tile_0, tile_1, free = tiles_of(places)
    copy_b.wait()
    extra = turned_rhs(b)
    copies_u[0].wait()
    copies_u[1].wait()
    lane = lax.broadcasted_iota(jnp.int32, extra.shape, 1)
    x[:, : 2 * RANK] = u[:, pl.ds(pl.multiple_of(2 * RANK * tile_0, 2 * RANK), 2 * RANK)]
    second = u[:, pl.ds(pl.multiple_of(2 * RANK * tile_1, 2 * RANK), 2 * RANK)]
    x[:, 2 * RANK :] = jnp.where(lane // RANK == free, extra, second)
    count = len(copies)
    starts = [sum(FEW_CHUNKS[:i]) for i in range(count + 1)]

    def gather(i, joined):
        total = mul(joined, v[starts[i] : starts[i + 1]])
        if i == 0:
            acc[: 4 * RANK + 16] = total
        else:
            acc[: 4 * RANK + 16] += total

    joined = None
    for i in range(count):
        copies[i].wait()
        if i == 1:
            copy_v.wait()
        middle = (starts[i] + starts[i + 1]) // 2
        ahead = [mul(d[starts[i] : middle], x[...]), mul(d[middle : starts[i + 1]], x[...])]
        if i > 0:
            gather(i - 1, joined)
        product = jnp.concatenate(ahead, axis=0)
        base = product[:, 2 * RANK :].T
        base = jnp.where(free == 1, base[RANK : RANK + 8], base[:8])
        _, low, rest = thirds(base)
        joined = jnp.concatenate([product.astype(bf16).T, low, rest], axis=0)
    copies_u[2].wait()
    gather(count - 1, joined)
    start = pl.multiple_of(2 * RANK + RANK * free, RANK)
    rhs[...] = acc[pl.ds(start, 8)] + acc[4 * RANK : 4 * RANK + 8] + acc[4 * RANK + 8 : 4 * RANK + 16]


def few_zeros(places, d, u, v, b, turned, z, acc, rhs, copies, copy_u, copy_b, copies_v):
    zeros = [places.nth(n, 0) for n in range(3)]
    starts = [sum(MANY_CHUNKS[:i]) for i in range(len(copies) + 1)]

    def turn(i):
        turned[:, starts[i] : starts[i + 1]] = v[starts[i] : starts[i + 1]].T

    copies_v[0].wait()
    turn(0)
    for i, c in enumerate(copies):
        c.wait()
        if i + 1 < len(copies):
            copies_v[i + 1].wait()
        part = slice(starts[i], starts[i + 1])
        rows = [turned[pl.ds(pl.multiple_of(RANK * n, RANK), RANK), part] for n in zeros]
        product = mul(jnp.concatenate(rows, axis=0), d[part])
        if i + 1 < len(copies):
            turn(i + 1)
        if i == 0:
            z[...] = product
        else:
            z[...] += product
    copy_b.wait()
    copy_u.wait()
    high, low = halves(z[...])
    both = jnp.concatenate([high, low], axis=0)
    product = mul(both, u[...])
    product = product[: 3 * RANK] + product[3 * RANK :]
    product = jnp.concatenate([product, jnp.zeros((RANK, STATE), f32)], axis=0)
    acc[:STATE, : 4 * RANK] = product.T
    twice = jnp.concatenate([b[...], b[...]], axis=0)
    shares = mul(twice, both, NT)[:8]
    shares = shares[:, : 3 * RANK] + shares[:, 3 * RANK :]
    pieces = []
    for k in range(LEVELS):
        before = k - places.ones_before[k]
        chosen = jnp.where(before == 1, shares[:, RANK : 2 * RANK], shares[:, :RANK])
        pieces.append(jnp.where(before == 2, shares[:, 2 * RANK :], chosen))
    rhs[...] = jnp.concatenate(pieces, axis=1)


def tiles_of(places):
    one_0, one_1 = places.nth(0, 1), places.nth(1, 1)
    one_0 = jnp.where(places.ones > 0, one_0, 0)
    one_1 = jnp.where(places.ones > 1, one_1, one_0)
    tile_0, tile_1 = one_0 // 2, one_1 // 2
    apart = tile_1 != tile_0
    free = jnp.where(apart, 1 - one_1 % 2, 0)
    tile_1 = jnp.where(apart, tile_1, (tile_0 + 1) % (LEVELS // 2))
    return tile_0, tile_1, free


def first_kernel(ranks, b_hbm, d_hbm, u_hbm, v_hbm, send, d, u, b, keeps, v, x, turned, z, acc, rhs, sems):
    n = max(len(FEW_CHUNKS), len(MANY_CHUNKS))

    def pieces_of(sizes):
        parts = [pl.ds(sum(sizes[:i]), sizes[i]) for i in range(len(sizes))]
        return [pltpu.make_async_copy(d_hbm.at[p], d.at[p], sems.at[i]) for i, p in enumerate(parts)]

    def pieces_of_v(sizes):
        parts = [pl.ds(sum(sizes[:i]), sizes[i]) for i in range(len(sizes))]
        return [pltpu.make_async_copy(v_hbm.at[p], v.at[p], sems.at[n + i]) for i, p in enumerate(parts)]

    places = Places(-1)
    few = places.ones <= 2
    tile_0, tile_1, _ = tiles_of(places)

    def tiles_of_u():
        parts = [
            pl.ds(pl.multiple_of(2 * RANK * t, 2 * RANK), 2 * RANK)
            for t in (tile_0, tile_1, LEVELS // 2 - tile_0 - tile_1)
        ]
        return [
            pltpu.make_async_copy(u_hbm.at[:, p], u.at[:, p], sems.at[2 * n + i]) for i, p in enumerate(parts)
        ]

    copy_u = pltpu.make_async_copy(u_hbm, u, sems.at[2 * n])
    copy_b = pltpu.make_async_copy(b_hbm, b, sems.at[2 * n + 3])
    copy_v = pltpu.make_async_copy(v_hbm, v, sems.at[n])

    @pl.when(few)
    def _():
        copies, tiles = pieces_of(FEW_CHUNKS), tiles_of_u()
        for c in (copy_b, *tiles[:2], copies[0], copy_v, *copies[1:], tiles[2]):
            c.start()

    @pl.when(jnp.logical_not(few))
    def _():
        for pair in zip(pieces_of_v(MANY_CHUNKS), pieces_of(MANY_CHUNKS)):
            for c in pair:
                c.start()
        copy_u.start()
        copy_b.start()

    plan = []
    for position in range(PIECES[0]):
        one, zero, valid = places.next_piece(position)
        m, l = places.nth(one, 1), places.nth(zero, 0)
        start = jnp.where(few, jnp.where(m // 2 == tile_0, 0, 2 * RANK) + RANK * (m % 2), RANK * m)
        lane_piece = jnp.where(few, l, jnp.minimum(zero, 2))
        plan.append((start, lane_piece, ranks[m], jnp.where(valid, ranks[l], 0)))
    keeps[...] = keep_row(ranks)

    @pl.when(few)
    def _():
        few_ones(places, d, u, v, b, x, acc, rhs, pieces_of(FEW_CHUNKS), tiles_of_u(), copy_b, copy_v)

    @pl.when(jnp.logical_not(few))
    def _():
        few_zeros(places, d, u, v, b, turned, z, acc, rhs, pieces_of(MANY_CHUNKS), copy_u, copy_b, pieces_of_v(MANY_CHUNKS))

    row_id = lax.broadcasted_iota(jnp.int32, (RANK, RANK), 0)
    lane_id = lax.broadcasted_iota(jnp.int32, (RANK, RANK), 1)
    for position, (start, lane_piece, rank_m, rank_l) in enumerate(plan):
        rows = pl.ds(pl.multiple_of(start, RANK), RANK)
        lanes = pl.ds(pl.multiple_of(2 * RANK * (lane_piece // 2), 2 * RANK), 2 * RANK)
        tile = acc[rows, lanes]
        block = jnp.where(lane_piece % 2 == 1, tile[:, RANK:], tile[:, :RANK])
        used = (row_id < rank_m) & (lane_id < rank_l)
        send[RANK // 2 * position : RANK // 2 * (position + 1)] = folded(jnp.where(used, block, 0.0))
    kept = rhs[...] * keeps[...]
    for tile in range(LEVELS // 2):
        row = RANK // 2 * PIECES[0] + 8 * tile
        send[row : row + 8] = kept[:, 2 * RANK * tile : 2 * RANK * (tile + 1)]


def mapped_kernel(half, d, u, b, keeps, mapped, base):
    size = d.shape[0] // 2
    joined = jnp.concatenate([u[...], turned_rhs(b)], axis=1)
    for i in range(size // CHUNK):
        part = slice(CHUNK * i, CHUNK * (i + 1))
        product = mul(d[size * half + CHUNK * i : size * half + CHUNK * (i + 1)], joined)
        mapped[:, part] = (product[:, :STATE] * keeps[:1]).astype(bf16).T
        base[:, part] = product[:, STATE:].T[:8]


def level_kernel(level, own, got, send, left):
    places = Places(level)
    is_upper = upper(level)
    count = PIECES[level]
    rhs_row = RANK // 2 * count
    tiles = LEVELS // 2 - level // 2
    lower_of = lambda index: unfolded(
        jnp.where(is_upper, piece(got, index, count), piece(own, index, count))
    )
    upper_of = lambda index: unfolded(
        jnp.where(is_upper, piece(own, index, count), piece(got, index, count))
    )
    own_rhs = jnp.concatenate([own[rhs_row + 8 * t : rhs_row + 8 * t + 8] for t in range(tiles)], axis=1)
    got_rhs = jnp.concatenate([got[rhs_row + 8 * t : rhs_row + 8 * t + 8] for t in range(tiles)], axis=1)
    skip = RANK * (level % 2)
    pivot_rhs = jnp.where(is_upper, got_rhs, own_rhs)[:, skip : skip + RANK]
    for position in range(PIECES[level + 1]):
        one, zero, valid = places.next_piece(position)
        index = one * places.zeros + zero
        product = wide_mul(lower_of(places.inner + one), upper_of(places.inner + zero))
        block = piece(own, index, count) + piece(got, index, count) - folded(product)
        send[RANK // 2 * position : RANK // 2 * (position + 1)] = jnp.where(valid, block, 0.0)
    rights = []
    lefts = []
    for k in range(places.count):
        zeros_before = k - places.ones_before[k]
        right = upper_of(places.inner + zeros_before)
        rights.append(jnp.where(places.bits[k] == 0, right, 0.0))
        theirs = unfolded(piece(got, places.inner + places.ones_before[k], count))
        lefts.append(jnp.where(is_upper & (places.bits[k] == 1), theirs, 0.0))
    blank = jnp.zeros((RANK, RANK + skip), f32)
    product = wide_mul(pivot_rhs, jnp.concatenate([blank, *rights], axis=1))
    rhs = own_rhs + got_rhs - product
    skip_tiles = level % 2
    for t in range(skip_tiles, tiles):
        row = RANK // 2 * PIECES[level + 1] + 8 * (t - skip_tiles)
        send[row : row + 8] = rhs[:, 2 * RANK * t : 2 * RANK * (t + 1)]
    lefts.append(jnp.where(is_upper, pivot_rhs, 0.0))
    left[...] = jnp.concatenate(lefts, axis=0)


def coefficients(left, t):
    if t is None:
        return -left
    return jnp.concatenate([t[RANK:] - wide_mul(left, t[:RANK]), -left], axis=1)


def coefficient_kernel(*refs):
    t = None
    for left in refs[:-1]:
        t = coefficients(left[...], t)
    refs[-1][...] = t


def basis_kernel(left, t_ref, mapped_0, mapped_1, base_0, base_1, out):
    t = coefficients(left[...], t_ref[...])
    w = jnp.concatenate([mapped_0[...], mapped_1[...]], axis=1)
    high, low = halves(t)
    rows = t.shape[0]
    product = mul(jnp.concatenate([high, low], axis=0), w[: t.shape[1]])
    product = product[:rows] + product[rows:]
    out[: 2 * RANK] = w[4 * RANK :].astype(f32) + product[: 2 * RANK]
    base = jnp.concatenate([base_0[...], base_1[...]], axis=1)
    out[2 * RANK :] = base + product[2 * RANK :]


def late_kernel(left, basis, high_low, shifted):
    update = basis[RANK:] - wide_mul(left[...], basis[:RANK])
    high, low = halves(update[:RANK])
    high_low[:RANK] = high
    high_low[RANK : 2 * RANK] = low
    high_low[2 * RANK :] = high
    shifted[...] = update[RANK:]


def last_kernel(got, high_low, shifted, out):
    value = jnp.where(upper(5), got[:, RANK:], 0.0)
    high, low = halves(value)
    out[...] = shifted[...] - mul(jnp.concatenate([high, high, low], axis=1), high_low[...])


def send_shape(level):
    return (RANK // 2 * PIECES[level] + 8 * (LEVELS // 2 - level // 2), 2 * RANK)


def call(kernel, name, outs, *args, after=()):
    vmem = pl.BlockSpec(memory_space=pltpu.VMEM)
    count = len(args)

    def body(*refs):
        kernel(*refs[:count], *refs[count + len(after) :])

    return pl.pallas_call(
        body,
        name=name,
        in_specs=[vmem] * count + [pl.BlockSpec(memory_space=pl.ANY)] * len(after),
        out_specs=[vmem] * len(outs),
        out_shape=[jax.ShapeDtypeStruct(s, t) for s, t in outs],
        compiler_params=pltpu.CompilerParams(vmem_limit_bytes=16 << 20),
    )(*args, *after)


def swapped(x, distance):
    return lax.ppermute(x, "leaf", [(i, i ^ distance) for i in range(lax.axis_size("leaf"))])


def on_device(rhs_vectors, diag_inverse, left_factors, right_factors, ranks):
    size = diag_inverse.shape[0]
    vmem = pl.BlockSpec(memory_space=pltpu.VMEM)
    hbm = pl.BlockSpec(memory_space=pltpu.HBM)
    send, d, u, b, keeps = pl.pallas_call(
        first_kernel,
        name="first",
        in_specs=[pl.BlockSpec(memory_space=pltpu.SMEM), hbm, hbm, hbm, hbm],
        out_specs=[vmem] * 5,
        out_shape=[
            jax.ShapeDtypeStruct(send_shape(0), f32),
            jax.ShapeDtypeStruct((size, size), bf16),
            jax.ShapeDtypeStruct((size, STATE), bf16),
            jax.ShapeDtypeStruct((8, size), bf16),
            jax.ShapeDtypeStruct((8, STATE), f32),
        ],
        scratch_shapes=[
            pltpu.VMEM((size, STATE), bf16),
            pltpu.VMEM((size, 4 * RANK), bf16),
            pltpu.VMEM((STATE, size), bf16),
            pltpu.VMEM((3 * RANK, size), f32),
            pltpu.VMEM((STATE, STATE), f32),
            pltpu.VMEM((8, STATE), f32),
            pltpu.SemaphoreType.DMA((2 * max(len(FEW_CHUNKS), len(MANY_CHUNKS)) + 4,)),
        ],
        compiler_params=pltpu.CompilerParams(vmem_limit_bytes=30 << 20),
    )(
        *(
            pltpu.with_memory_space_constraint(a, pltpu.HBM)
            for a in (ranks, rhs_vectors, diag_inverse, left_factors, right_factors)
        ),
    )
    mapped = []
    lefts = []
    basis = t = None
    for level in range(LEVELS - 1):
        got = swapped(send, PARTNER[level])
        after = ()
        if level in (1, 2):
            after = call(
                lambda *refs, half=level - 1: mapped_kernel(half, *refs),
                f"mapped_{level}",
                [((STATE, size // 2), bf16), ((8, size // 2), f32)],
                d,
                u,
                b,
                keeps,
                after=(send,),
            )
            mapped.append(after)
        if level == 3:
            (t,) = after = call(coefficient_kernel, "coefficients", [((3 * RANK + 8, 3 * RANK), f32)], *lefts)
        if level == 4:
            (basis,) = after = call(
                basis_kernel, "basis", [((2 * RANK + 8, size), f32)], lefts[3], t, *(m[0] for m in mapped), *(m[1] for m in mapped)
            )
        send, left = call(
            lambda *refs, level=level: level_kernel(level, *refs),
            f"level_{level}",
            [(send_shape(level + 1), f32), ((RANK * (LEVELS - 1 - level) + 8, RANK), f32)],
            send,
            got,
            after=after,
        )
        lefts.append(left)
    got = swapped(send, PARTNER[LEVELS - 1])
    high_low, shifted = call(
        late_kernel, "late", [((3 * RANK, size), bf16), ((8, size), f32)], lefts[4], basis
    )
    (out,) = call(last_kernel, "last", [((8, size), f32)], got, high_low, shifted)
    return out


def solution(mesh):
    in_specs = (P("rhs", "leaf"), P("leaf", None), P("leaf", None), P("leaf", None), P())
    out_specs = P("rhs", "leaf")
    return jax.shard_map(
        on_device, mesh=mesh, in_specs=in_specs, out_specs=out_specs, check_vma=False
    )
```

```python
import jax
import jax.numpy as jnp
from jax import lax
from jax.experimental import pallas as pl
from jax.experimental.pallas import tpu as pltpu
from jax.sharding import PartitionSpec as P

f32 = jnp.float32
bf16 = jnp.bfloat16
NN = (((1,), (0,)), ((), ()))
NT = (((1,), (1,)), ((), ()))
RANK = 64
LEVELS = 6
STATE = RANK * LEVELS
CHUNK = 512
FEW_CHUNKS = (512, 512, 512, 512)
MANY_CHUNKS = (256, 256, 512, 512, 512)
PARTNER = (1, 2, 4, 12, 16, 48)
PIECES = (9, 6, 4, 2, 1, 0)


def mul(a, b, dims=NN):
    return lax.dot_general(a, b, dims, preferred_element_type=f32)


def halves(x):
    high = x.astype(bf16)
    return high, (x - high.astype(f32)).astype(bf16)


def thirds(x):
    high, low = halves(x)
    rest = x - high.astype(f32) - low.astype(f32)
    return high, low, rest.astype(bf16)


def wide_mul(a, b):
    a_high, a_low = halves(a)
    b_high, b_low = halves(b)
    return mul(
        jnp.concatenate([a_high, a_high, a_low], axis=1),
        jnp.concatenate([b_high, b_low, b_high], axis=0),
    )


def upper(level):
    return (lax.axis_index("leaf") >> level & 1) == 1


def folded(x):
    return jnp.concatenate([x[: RANK // 2], x[RANK // 2 :]], axis=1)


def unfolded(x):
    return jnp.concatenate([x[:, :RANK], x[:, RANK:]], axis=0)


class Places:
    def __init__(self, level):
        self.count = LEVELS - 1 - level
        leaf = lax.axis_index("leaf")
        self.bits = [(leaf >> (level + 1 + k)) & 1 for k in range(self.count)]
        self.ones_before = [sum(self.bits[:k], jnp.int32(0)) for k in range(self.count + 1)]
        self.ones = self.ones_before[-1]
        self.zeros = self.count - self.ones
        self.inner = self.ones * self.zeros

    def next_piece(self, position):
        own = self.bits[0]
        ones, zeros = self.ones - own, self.zeros - (1 - own)
        inner = ones * zeros
        within = position < inner
        a = sum([(position >= t * zeros).astype(jnp.int32) for t in range(1, self.count)], jnp.int32(0))
        b = position - a * zeros
        rest = position - inner
        a = jnp.where(within, a + own, jnp.where(own == 1, 0, rest))
        b = jnp.where(within, b + 1 - own, jnp.where(own == 1, rest, 0))
        valid = (a < self.ones) & (b < self.zeros)
        return jnp.where(valid, a, 0), jnp.where(valid, b, 0), valid

    def nth(self, n, bit):
        found = jnp.int32(0)
        for k in range(self.count):
            before = self.ones_before[k] if bit else k - self.ones_before[k]
            found = jnp.where((before == n) & (self.bits[k] == bit), k, found)
        return found


def piece(ref, index, limit):
    index = jnp.minimum(index, limit - 1)
    return ref[pl.ds(pl.multiple_of(RANK // 2 * index, RANK // 2), RANK // 2)]


def keep_row(ranks):
    lane = lax.broadcasted_iota(jnp.int32, (8, STATE), 1)
    keep = jnp.zeros((8, STATE), f32)
    for level in range(LEVELS):
        inside = (lane >= RANK * level) & (lane < RANK * level + jnp.minimum(ranks[level], RANK))
        keep = jnp.where(inside, 1.0, keep)
    return keep


def turned_rhs(b):
    wide = b[...].astype(f32)
    gap = jnp.zeros((RANK - 8, wide.shape[1]), f32)
    return jnp.concatenate([wide, gap, wide, gap], axis=0).T.astype(bf16)


def few_ones(places, d, u, v, b, x, acc, rhs, copies, copies_u, copy_b, copy_v):
    tile_0, tile_1, free = tiles_of(places)
    copy_b.wait()
    extra = turned_rhs(b)
    copies_u[0].wait()
    copies_u[1].wait()
    lane = lax.broadcasted_iota(jnp.int32, extra.shape, 1)
    x[:, : 2 * RANK] = u[:, pl.ds(pl.multiple_of(2 * RANK * tile_0, 2 * RANK), 2 * RANK)]
    second = u[:, pl.ds(pl.multiple_of(2 * RANK * tile_1, 2 * RANK), 2 * RANK)]
    x[:, 2 * RANK :] = jnp.where(lane // RANK == free, extra, second)
    count = len(copies)
    starts = [sum(FEW_CHUNKS[:i]) for i in range(count + 1)]

    def gather(i, joined):
        total = mul(joined, v[starts[i] : starts[i + 1]])
        if i == 0:
            acc[: 4 * RANK + 16] = total
        else:
            acc[: 4 * RANK + 16] += total

    joined = None
    for i in range(count):
        copies[i].wait()
        if i == 1:
            copy_v.wait()
        middle = (starts[i] + starts[i + 1]) // 2
        ahead = [mul(d[starts[i] : middle], x[...]), mul(d[middle : starts[i + 1]], x[...])]
        if i > 0:
            gather(i - 1, joined)
        product = jnp.concatenate(ahead, axis=0)
        base = product[:, 2 * RANK :].T
        base = jnp.where(free == 1, base[RANK : RANK + 8], base[:8])
        _, low, rest = thirds(base)
        joined = jnp.concatenate([product.astype(bf16).T, low, rest], axis=0)
    copies_u[2].wait()
    gather(count - 1, joined)
    start = pl.multiple_of(2 * RANK + RANK * free, RANK)
    rhs[...] = acc[pl.ds(start, 8)] + acc[4 * RANK : 4 * RANK + 8] + acc[4 * RANK + 8 : 4 * RANK + 16]


def few_zeros(places, d, u, v, b, turned, z, acc, rhs, copies, copy_u, copy_b, copies_v):
    zeros = [places.nth(n, 0) for n in range(3)]
    starts = [sum(MANY_CHUNKS[:i]) for i in range(len(copies) + 1)]

    def turn(i):
        turned[:, starts[i] : starts[i + 1]] = v[starts[i] : starts[i + 1]].T

    copies_v[0].wait()
    turn(0)
    for i, c in enumerate(copies):
        c.wait()
        if i + 1 < len(copies):
            copies_v[i + 1].wait()
        part = slice(starts[i], starts[i + 1])
        rows = [turned[pl.ds(pl.multiple_of(RANK * n, RANK), RANK), part] for n in zeros]
        product = mul(jnp.concatenate(rows, axis=0), d[part])
        if i + 1 < len(copies):
            turn(i + 1)
        if i == 0:
            z[...] = product
        else:
            z[...] += product
    copy_b.wait()
    copy_u.wait()
    high, low = halves(z[...])
    both = jnp.concatenate([high, low], axis=0)
    product = mul(both, u[...])
    product = product[: 3 * RANK] + product[3 * RANK :]
    product = jnp.concatenate([product, jnp.zeros((RANK, STATE), f32)], axis=0)
    acc[:STATE, : 4 * RANK] = product.T
    twice = jnp.concatenate([b[...], b[...]], axis=0)
    shares = mul(twice, both, NT)[:8]
    shares = shares[:, : 3 * RANK] + shares[:, 3 * RANK :]
    pieces = []
    for k in range(LEVELS):
        before = k - places.ones_before[k]
        chosen = jnp.where(before == 1, shares[:, RANK : 2 * RANK], shares[:, :RANK])
        pieces.append(jnp.where(before == 2, shares[:, 2 * RANK :], chosen))
    rhs[...] = jnp.concatenate(pieces, axis=1)


def tiles_of(places):
    one_0, one_1 = places.nth(0, 1), places.nth(1, 1)
    one_0 = jnp.where(places.ones > 0, one_0, 0)
    one_1 = jnp.where(places.ones > 1, one_1, one_0)
    tile_0, tile_1 = one_0 // 2, one_1 // 2
    apart = tile_1 != tile_0
    free = jnp.where(apart, 1 - one_1 % 2, 0)
    tile_1 = jnp.where(apart, tile_1, (tile_0 + 1) % (LEVELS // 2))
    return tile_0, tile_1, free


def first_kernel(ranks, b_hbm, d_hbm, u_hbm, v_hbm, send, d, u, b, keeps, v, x, turned, z, acc, rhs, plan, sems):
    n = max(len(FEW_CHUNKS), len(MANY_CHUNKS))

    def pieces_of(sizes):
        parts = [pl.ds(sum(sizes[:i]), sizes[i]) for i in range(len(sizes))]
        return [pltpu.make_async_copy(d_hbm.at[p], d.at[p], sems.at[i]) for i, p in enumerate(parts)]

    def pieces_of_v(sizes):
        parts = [pl.ds(sum(sizes[:i]), sizes[i]) for i in range(len(sizes))]
        return [pltpu.make_async_copy(v_hbm.at[p], v.at[p], sems.at[n + i]) for i, p in enumerate(parts)]

    places = Places(-1)
    few = places.ones <= 2
    tile_0, tile_1, _ = tiles_of(places)

    def tiles_of_u():
        parts = [
            pl.ds(pl.multiple_of(2 * RANK * t, 2 * RANK), 2 * RANK)
            for t in (tile_0, tile_1, LEVELS // 2 - tile_0 - tile_1)
        ]
        return [
            pltpu.make_async_copy(u_hbm.at[:, p], u.at[:, p], sems.at[2 * n + i]) for i, p in enumerate(parts)
        ]

    copy_u = pltpu.make_async_copy(u_hbm, u, sems.at[2 * n])
    copy_b = pltpu.make_async_copy(b_hbm, b, sems.at[2 * n + 3])
    copy_v = pltpu.make_async_copy(v_hbm, v, sems.at[n])

    @pl.when(few)
    def _():
        copies, tiles = pieces_of(FEW_CHUNKS), tiles_of_u()
        for c in (copy_b, *tiles[:2], copies[0], copy_v, *copies[1:], tiles[2]):
            c.start()

    @pl.when(jnp.logical_not(few))
    def _():
        for pair in zip(pieces_of_v(MANY_CHUNKS), pieces_of(MANY_CHUNKS)):
            for c in pair:
                c.start()
        copy_u.start()
        copy_b.start()

    def write_plan(few):
        for position in range(PIECES[0]):
            one, zero, valid = places.next_piece(position)
            m, l = places.nth(one, 1), places.nth(zero, 0)
            if few:
                plan[4 * position] = jnp.where(m // 2 == tile_0, 0, 2 * RANK) + RANK * (m % 2)
                plan[4 * position + 1] = l
            else:
                plan[4 * position] = RANK * m
                plan[4 * position + 1] = jnp.minimum(zero, 2)
            plan[4 * position + 2] = ranks[m]
            plan[4 * position + 3] = jnp.where(valid, ranks[l], 0)
        keeps[...] = keep_row(ranks)

    @pl.when(few)
    def _():
        write_plan(True)
        few_ones(places, d, u, v, b, x, acc, rhs, pieces_of(FEW_CHUNKS), tiles_of_u(), copy_b, copy_v)

    @pl.when(jnp.logical_not(few))
    def _():
        write_plan(False)
        few_zeros(places, d, u, v, b, turned, z, acc, rhs, pieces_of(MANY_CHUNKS), copy_u, copy_b, pieces_of_v(MANY_CHUNKS))

    row_id = lax.broadcasted_iota(jnp.int32, (RANK, RANK), 0)
    lane_id = lax.broadcasted_iota(jnp.int32, (RANK, RANK), 1)
    for position in range(PIECES[0]):
        start, lane_piece, rank_m, rank_l = [plan[4 * position + k] for k in range(4)]
        rows = pl.ds(pl.multiple_of(start, RANK), RANK)
        lanes = pl.ds(pl.multiple_of(2 * RANK * (lane_piece // 2), 2 * RANK), 2 * RANK)
        tile = acc[rows, lanes]
        block = jnp.where(lane_piece % 2 == 1, tile[:, RANK:], tile[:, :RANK])
        used = (row_id < rank_m) & (lane_id < rank_l)
        send[RANK // 2 * position : RANK // 2 * (position + 1)] = folded(jnp.where(used, block, 0.0))
    kept = rhs[...] * keeps[...]
    for tile in range(LEVELS // 2):
        row = RANK // 2 * PIECES[0] + 8 * tile
        send[row : row + 8] = kept[:, 2 * RANK * tile : 2 * RANK * (tile + 1)]


def mapped_kernel(half, d, u, b, keeps, mapped, base):
    size = d.shape[0] // 2
    joined = jnp.concatenate([u[...], turned_rhs(b)], axis=1)
    for i in range(size // CHUNK):
        part = slice(CHUNK * i, CHUNK * (i + 1))
        product = mul(d[size * half + CHUNK * i : size * half + CHUNK * (i + 1)], joined)
        mapped[:, part] = (product[:, :STATE] * keeps[:1]).astype(bf16).T
        base[:, part] = product[:, STATE:].T[:8]


def level_kernel(level, own, got, send, left):
    places = Places(level)
    is_upper = upper(level)
    count = PIECES[level]
    rhs_row = RANK // 2 * count
    tiles = LEVELS // 2 - level // 2
    lower_of = lambda index: unfolded(
        jnp.where(is_upper, piece(got, index, count), piece(own, index, count))
    )
    upper_of = lambda index: unfolded(
        jnp.where(is_upper, piece(own, index, count), piece(got, index, count))
    )
    own_rhs = jnp.concatenate([own[rhs_row + 8 * t : rhs_row + 8 * t + 8] for t in range(tiles)], axis=1)
    got_rhs = jnp.concatenate([got[rhs_row + 8 * t : rhs_row + 8 * t + 8] for t in range(tiles)], axis=1)
    skip = RANK * (level % 2)
    pivot_rhs = jnp.where(is_upper, got_rhs, own_rhs)[:, skip : skip + RANK]
    for position in range(PIECES[level + 1]):
        one, zero, valid = places.next_piece(position)
        index = one * places.zeros + zero
        product = wide_mul(lower_of(places.inner + one), upper_of(places.inner + zero))
        block = piece(own, index, count) + piece(got, index, count) - folded(product)
        send[RANK // 2 * position : RANK // 2 * (position + 1)] = jnp.where(valid, block, 0.0)
    rights = []
    lefts = []
    for k in range(places.count):
        zeros_before = k - places.ones_before[k]
        right = upper_of(places.inner + zeros_before)
        rights.append(jnp.where(places.bits[k] == 0, right, 0.0))
        theirs = unfolded(piece(got, places.inner + places.ones_before[k], count))
        lefts.append(jnp.where(is_upper & (places.bits[k] == 1), theirs, 0.0))
    blank = jnp.zeros((RANK, RANK + skip), f32)
    product = wide_mul(pivot_rhs, jnp.concatenate([blank, *rights], axis=1))
    rhs = own_rhs + got_rhs - product
    skip_tiles = level % 2
    for t in range(skip_tiles, tiles):
        row = RANK // 2 * PIECES[level + 1] + 8 * (t - skip_tiles)
        send[row : row + 8] = rhs[:, 2 * RANK * t : 2 * RANK * (t + 1)]
    lefts.append(jnp.where(is_upper, pivot_rhs, 0.0))
    left[...] = jnp.concatenate(lefts, axis=0)


def coefficients(left, t):
    if t is None:
        return -left
    return jnp.concatenate([t[RANK:] - wide_mul(left, t[:RANK]), -left], axis=1)


def coefficient_kernel(*refs):
    t = None
    for left in refs[:-1]:
        t = coefficients(left[...], t)
    refs[-1][...] = t


def basis_kernel(left, t_ref, mapped_0, mapped_1, base_0, base_1, out):
    t = coefficients(left[...], t_ref[...])
    w = jnp.concatenate([mapped_0[...], mapped_1[...]], axis=1)
    high, low = halves(t)
    rows = t.shape[0]
    product = mul(jnp.concatenate([high, low], axis=0), w[: t.shape[1]])
    product = product[:rows] + product[rows:]
    out[: 2 * RANK] = w[4 * RANK :].astype(f32) + product[: 2 * RANK]
    base = jnp.concatenate([base_0[...], base_1[...]], axis=1)
    out[2 * RANK :] = base + product[2 * RANK :]


def late_kernel(left, basis, high_low, shifted):
    update = basis[RANK:] - wide_mul(left[...], basis[:RANK])
    high, low = halves(update[:RANK])
    high_low[:RANK] = high
    high_low[RANK : 2 * RANK] = low
    high_low[2 * RANK :] = high
    shifted[...] = update[RANK:]


def last_kernel(got, high_low, shifted, out):
    value = jnp.where(upper(5), got[:, RANK:], 0.0)
    high, low = halves(value)
    out[...] = shifted[...] - mul(jnp.concatenate([high, high, low], axis=1), high_low[...])


def send_shape(level):
    return (RANK // 2 * PIECES[level] + 8 * (LEVELS // 2 - level // 2), 2 * RANK)


def call(kernel, name, outs, *args, after=()):
    vmem = pl.BlockSpec(memory_space=pltpu.VMEM)
    count = len(args)

    def body(*refs):
        kernel(*refs[:count], *refs[count + len(after) :])

    return pl.pallas_call(
        body,
        name=name,
        in_specs=[vmem] * count + [pl.BlockSpec(memory_space=pl.ANY)] * len(after),
        out_specs=[vmem] * len(outs),
        out_shape=[jax.ShapeDtypeStruct(s, t) for s, t in outs],
        compiler_params=pltpu.CompilerParams(vmem_limit_bytes=16 << 20),
    )(*args, *after)


def swapped(x, distance):
    return lax.ppermute(x, "leaf", [(i, i ^ distance) for i in range(lax.axis_size("leaf"))])


def on_device(rhs_vectors, diag_inverse, left_factors, right_factors, ranks):
    size = diag_inverse.shape[0]
    vmem = pl.BlockSpec(memory_space=pltpu.VMEM)
    hbm = pl.BlockSpec(memory_space=pltpu.HBM)
    send, d, u, b, keeps = pl.pallas_call(
        first_kernel,
        name="first",
        in_specs=[pl.BlockSpec(memory_space=pltpu.SMEM), hbm, hbm, hbm, hbm],
        out_specs=[vmem] * 5,
        out_shape=[
            jax.ShapeDtypeStruct(send_shape(0), f32),
            jax.ShapeDtypeStruct((size, size), bf16),
            jax.ShapeDtypeStruct((size, STATE), bf16),
            jax.ShapeDtypeStruct((8, size), bf16),
            jax.ShapeDtypeStruct((8, STATE), f32),
        ],
        scratch_shapes=[
            pltpu.VMEM((size, STATE), bf16),
            pltpu.VMEM((size, 4 * RANK), bf16),
            pltpu.VMEM((STATE, size), bf16),
            pltpu.VMEM((3 * RANK, size), f32),
            pltpu.VMEM((STATE, STATE), f32),
            pltpu.VMEM((8, STATE), f32),
            pltpu.SMEM((4 * PIECES[0],), jnp.int32),
            pltpu.SemaphoreType.DMA((2 * max(len(FEW_CHUNKS), len(MANY_CHUNKS)) + 4,)),
        ],
        compiler_params=pltpu.CompilerParams(vmem_limit_bytes=30 << 20),
    )(
        *(
            pltpu.with_memory_space_constraint(a, pltpu.HBM)
            for a in (ranks, rhs_vectors, diag_inverse, left_factors, right_factors)
        ),
    )
    mapped = []
    lefts = []
    basis = t = None
    for level in range(LEVELS - 1):
        got = swapped(send, PARTNER[level])
        after = ()
        if level in (1, 2):
            after = call(
                lambda *refs, half=level - 1: mapped_kernel(half, *refs),
                f"mapped_{level}",
                [((STATE, size // 2), bf16), ((8, size // 2), f32)],
                d,
                u,
                b,
                keeps,
                after=(send,),
            )
            mapped.append(after)
        if level == 3:
            (t,) = after = call(coefficient_kernel, "coefficients", [((3 * RANK + 8, 3 * RANK), f32)], *lefts)
        if level == 4:
            (basis,) = after = call(
                basis_kernel, "basis", [((2 * RANK + 8, size), f32)], lefts[3], t, *(m[0] for m in mapped), *(m[1] for m in mapped)
            )
        send, left = call(
            lambda *refs, level=level: level_kernel(level, *refs),
            f"level_{level}",
            [(send_shape(level + 1), f32), ((RANK * (LEVELS - 1 - level) + 8, RANK), f32)],
            send,
            got,
            after=after,
        )
        lefts.append(left)
    got = swapped(send, PARTNER[LEVELS - 1])
    high_low, shifted = call(
        late_kernel, "late", [((3 * RANK, size), bf16), ((8, size), f32)], lefts[4], basis
    )
    (out,) = call(last_kernel, "last", [((8, size), f32)], got, high_low, shifted)
    return out


def solution(mesh):
    in_specs = (P("rhs", "leaf"), P("leaf", None), P("leaf", None), P("leaf", None), P())
    out_specs = P("rhs", "leaf")
    return jax.shard_map(
        on_device, mesh=mesh, in_specs=in_specs, out_specs=out_specs, check_vma=False
    )
```
